32 devices in a mesh: groups: 2 (over x), ctx: 16 (over z, y, core).
Axes of the slice: x: 2, y: 2, z: 4, core: 2. Of those that a mesh axis runs over, the one named last changes fastest.
Arguments:
- query_input: bfloat16 [32, 1536], P('groups'), parts along dimension 0, may hold values from -20 to 20
- query_gain: bfloat16 [1536], replicated, may hold values from 0.5 to 1.5
- nope_weight: bfloat16 [1536, 4096], P(None, 'ctx'), may hold values from -0.15625 to 0.15625
- rope_weight: bfloat16 [1536, 2048], P(None, 'ctx'), may hold values from -0.15625 to 0.15625
- key_up: bfloat16 [32, 128, 512], P('ctx'), may hold values from -0.5 to 0.5
- value_up: bfloat16 [32, 512, 128], P('ctx'), may hold values from -1 to 1
- out_weight: bfloat16 [4096, 7168], P('ctx'), may hold values from -0.09375 to 0.09375
- cache_latent: bfloat16 [4, 32768, 512], P('groups', 'ctx'), parts along dimension 0, may hold values from -8 to 8
- cache_rope: bfloat16 [4, 64, 32768], P('groups', None, 'ctx'), parts along dimension 0, may hold values from -256 to 256
- cached_length: int32 [4], P('groups'), parts along dimension 0, may hold values from 16384 to 32760, as said below
Outputs:
- attn_out: bfloat16 [32, 7168], P('groups'), parts along dimension 0
The draws below stay inside these ranges and needn't reach their ends.
There are 2 independent parts, one for each index of `groups`. The reference program is written for one: setup_inputs(seed, part) draws one part's arguments, and reference() takes and returns one part's arrays. A program takes and returns all parts, laid end to end along the dimension named above; an argument that names none is the same for every part. Nothing has to cross between parts.
Inputs may be any that keep to these rules, and one draw needn't show every extreme that they name: `cached_length`: in every part one request has exactly 32760, so that its last new token sees the cache's last position.
All inputs are finite; a program needn't handle non-finite values.
Results may differ from the reference program's by a relative error of at most 0.012.
Values may be sent and summed in bfloat16 or wider, within the bound.
A program may use at most 128 MiB of HBM per device.

```python
import math
import jax
import jax.numpy as jnp
from jax import lax

D = 7168
QR = 1536
NOPE = 128
ROPE = 64
LAT = 512
VDIM = 128
REQS = 2
STRETCH = 8
CTX_DEV = 2048
HEADS = 32
ROWS = 16
CACHE = 32768
N_CTX = 16


def key_scales(key, smallest, widest):
    spread = jax.random.uniform(jax.random.fold_in(key, 11), (REQS, CACHE), jnp.float32)
    return jnp.exp(jnp.log(smallest) + spread * jnp.log(widest))


def latent_region(key):
    mode_count = 2 * (CACHE // CTX_DEV)
    phases = jax.random.uniform(jax.random.fold_in(key, 13), (REQS, 1, mode_count), jnp.float32) * (2.0 * math.pi)
    vectors = jax.random.normal(jax.random.fold_in(key, 14), (REQS, mode_count, LAT), jnp.float32)
    frequency = (jnp.arange(mode_count, dtype=jnp.float32) + 1.0) * (math.pi / CACHE)
    position = jnp.arange(CACHE, dtype=jnp.float32)
    wave_table = jnp.cos(position[None, :, None] * frequency[None, None, :] + phases) * math.sqrt(2.0 / mode_count)
    return jnp.einsum('bpk,bkl->bpl', wave_table, vectors)


def draw_query_input(key, part):
    spread = jax.random.uniform(jax.random.fold_in(key, 41), (ROWS, 1), jnp.float32)
    row_scale = jnp.exp(jnp.log(0.3) + spread * jnp.log(10.0))
    entries = jax.random.normal(jax.random.fold_in(key, 42), (ROWS, QR), jnp.float32)
    return jnp.clip(entries * row_scale, -20.0, 20.0).astype(jnp.bfloat16)


def draw_cache_latent(key, part):
    scales = key_scales(key, 0.08, 5.0)
    entries = jax.random.normal(jax.random.fold_in(key, 21), (REQS, CACHE, LAT), jnp.float32)
    scaled = (entries + latent_region(key)) * scales[:, :, None]
    return jnp.clip(scaled, -8.0, 8.0).astype(jnp.bfloat16)


def draw_cache_rope(key, part):
    chosen = jax.random.randint(jax.random.fold_in(key, 32), (REQS, 8), 0, CACHE // 2)
    marked = jnp.any(jnp.arange(CACHE, dtype=jnp.int32)[None, None, :] == chosen[:, :, None], axis=1)
    sink_strength = 0.65 * math.log(CACHE)
    scales = key_scales(key, 0.08, 5.0)
    entries = jax.random.normal(jax.random.fold_in(key, 31), (REQS, ROPE, CACHE), jnp.float32)
    scaled = jnp.where(marked[:, None, :], entries * sink_strength, entries * scales[:, None, :])
    return jnp.clip(scaled, -256.0, 256.0).astype(jnp.bfloat16)


def draw_cached_length(key, part):
    longest = jax.random.randint(jax.random.fold_in(key, 51), (), 0, REQS)
    others = jax.random.randint(jax.random.fold_in(key, 52), (REQS,), CACHE // 2, CACHE - STRETCH + 1)
    return jnp.where(jnp.arange(REQS, dtype=jnp.int32) == longest, CACHE - STRETCH, others).astype(jnp.int32)


def block_scale(stream_key, extent, cuts, low, high):
    loudness, own = 1.0, jax.random.fold_in(stream_key, 6)
    for axis_at, blocks in cuts:
        heights = jnp.exp(jax.random.uniform(jax.random.fold_in(own, axis_at), (blocks,), jnp.float32, low / len(cuts), high / len(cuts)))
        loudness = loudness * jnp.repeat(heights, extent[axis_at] // blocks).reshape([-1 if axis == axis_at else 1 for axis in range(len(extent))])
    return loudness


def noise(key, extent, width, most, split=(), held_as=jnp.bfloat16):
    factor_of = block_scale(key, extent, split, -0.22, 0.18) if split else 1.0
    result = jax.random.normal(key, extent, jnp.float32) * width * factor_of
    return jnp.minimum(jnp.maximum(result, -most), most).astype(held_as)


def setup_inputs(seed: int = 0, part: int = 0) -> dict:
    splits = jax.random.split(jax.random.key(seed), 11)
    part_keys = jax.random.split(jax.random.fold_in(splits[10], part), 11)
    return {
        "query_input": draw_query_input(jax.random.fold_in(jax.random.fold_in(splits[10], part), 71), part),
        "query_gain": jnp.clip(1.0 + 0.1 * jax.random.normal(splits[1], (QR,), jnp.float32), 0.5, 1.5).astype(jnp.bfloat16),
        "nope_weight": noise(splits[2], (QR, HEADS * NOPE), QR ** -0.5, 0.15625, ((1, 16),)),
        "rope_weight": noise(splits[3], (QR, HEADS * ROPE), QR ** -0.5, 0.15625, ((1, 16),)),
        "key_up": noise(splits[4], (HEADS, NOPE, LAT), NOPE ** -0.5, 0.5, ((0, 16),)),
        "value_up": noise(splits[5], (HEADS, LAT, VDIM), (LAT // 16) ** -0.5, 1.0, ((0, 16),)),
        "out_weight": noise(splits[6], (HEADS * VDIM, D), (HEADS * VDIM) ** -0.5, 0.09375, ((0, 16),)),
        "cache_latent": draw_cache_latent(jax.random.fold_in(jax.random.fold_in(splits[10], part), 71), part),
        "cache_rope": draw_cache_rope(jax.random.fold_in(jax.random.fold_in(splits[10], part), 71), part),
        "cached_length": draw_cached_length(jax.random.fold_in(jax.random.fold_in(splits[10], part), 71), part),
    }


mscale_yarn = 1.0 + 0.1 * math.log(40.0)
masked_score = -1e+30

def reference(query_input, query_gain, nope_weight, rope_weight, key_up, value_up, out_weight, cache_latent, cache_rope, cached_length):
    widened = query_input.astype(jnp.float32)
    normed = (widened * lax.rsqrt(lax.optimization_barrier(jnp.mean(widened * widened, axis=-1, keepdims=True)) + 1e-06) * query_gain.astype(jnp.float32)).astype(jnp.bfloat16)
    query_nope = jnp.dot(normed, nope_weight, preferred_element_type=jnp.float32).astype(jnp.bfloat16).reshape(ROWS, HEADS, NOPE)
    query_rope = jnp.dot(normed, rope_weight, preferred_element_type=jnp.float32).astype(jnp.bfloat16).reshape(ROWS, HEADS, ROPE)
    query_latent = jnp.einsum('rhn,hnl->rhl', query_nope.astype(jnp.float32), key_up.astype(jnp.float32)).astype(jnp.bfloat16)
    softmax_scale = mscale_yarn * mscale_yarn / math.sqrt(NOPE + ROPE)
    latent_rows = query_latent.astype(jnp.float32).reshape(REQS, STRETCH, HEADS, LAT)
    rope_rows = query_rope.astype(jnp.float32).reshape(REQS, STRETCH, HEADS, ROPE)
    last_seen = cached_length.astype(jnp.int32)[:, None] + jnp.arange(STRETCH, dtype=jnp.int32)[None, :]

    def one_block(running, block):
        row_top, weight_sum, pooled = running
        first_key = (block * CTX_DEV).astype(jnp.int32)
        key_block = lax.dynamic_slice_in_dim(cache_latent, first_key, CTX_DEV, 1).astype(jnp.float32)
        rope_block = lax.dynamic_slice_in_dim(cache_rope, first_key, CTX_DEV, 2).astype(jnp.float32)
        positions = first_key + jnp.arange(CTX_DEV, dtype=jnp.int32)
        scores = softmax_scale * (jnp.einsum('bchl,bpl->bchp', latent_rows, key_block) + jnp.einsum('bche,bep->bchp', rope_rows, rope_block))
        visible = (positions[None, None, :] <= last_seen[:, :, None])[:, :, None, :]
        scores = jnp.where(visible, scores, masked_score)
        block_peak = lax.optimization_barrier(jnp.max(scores, axis=-1))
        weights = jnp.where(visible, jnp.exp(scores - block_peak[..., None]), 0.0)
        rounded = lax.optimization_barrier(weights.astype(jnp.bfloat16)).astype(jnp.float32)
        block_sum = lax.optimization_barrier(jnp.sum(weights, axis=-1))
        block_pool = jnp.einsum('bchp,bpl->bchl', rounded, key_block)
        new_top = jnp.maximum(row_top, block_peak)
        keep_old = jnp.exp(row_top - new_top)
        keep_new = jnp.exp(block_peak - new_top)
        weight_sum = weight_sum * keep_old + block_sum * keep_new
        pooled = pooled * keep_old[..., None] + block_pool * keep_new[..., None]
        return ((new_top, weight_sum, pooled), None)
    initial = (jnp.full((REQS, STRETCH, HEADS), masked_score, jnp.float32), jnp.zeros((REQS, STRETCH, HEADS), jnp.float32), jnp.zeros((REQS, STRETCH, HEADS, LAT), jnp.float32))
    finals, unused = lax.scan(one_block, initial, jnp.arange(N_CTX, dtype=jnp.int32))
    row_top, weight_sum, pooled = finals
    attended = (pooled / weight_sum[..., None]).astype(jnp.bfloat16).reshape(ROWS, HEADS, LAT)
    head_values = jnp.einsum('rhl,hlv->rhv', attended.astype(jnp.float32), value_up.astype(jnp.float32)).astype(jnp.bfloat16).reshape(ROWS, HEADS * VDIM)
    return jnp.dot(head_values, out_weight, preferred_element_type=jnp.float32).astype(jnp.bfloat16)
```

```python
import functools
import math

import jax
import jax.numpy as jnp
from jax import lax
from jax.experimental import pallas as pl
from jax.experimental.pallas import tpu as pltpu
from jax.sharding import PartitionSpec as P

mscale_yarn = 1.0 + 0.1 * math.log(40.0)
masked_score = -1e30
MESH = pl.DeviceIdType.MESH
F32 = jnp.float32
BF16 = jnp.bfloat16
NT = (((1,), (1,)), ((), ()))


def pieces(value):
    out = []
    for _ in range(3):
        piece = value.astype(BF16).astype(F32)
        out.append(piece)
        value = value - piece
    return out


def kernel(
    n, tile, chunk,
    x_hbm, gain_hbm, nope_hbm, ropew_hbm, kup_hbm, vup_hbm, outw_hbm, lat_hbm, crope_hbm, len_hbm,
    out_ref,
    x_v, gain_v, nope_v, ropew_v, kup_v, vup_v, outw_v, lat_v, crope_v, len_s,
    qbuf, score_s, stat_s, pool_s, sb, rb, hvbuf, opart, ob, orb, fin,
    ld_sem,
    kvs, kvr, qs, qr, ps, pr, hs, hr, os, orr, fs, fr, gs, gr,
):
    me = lax.axis_index("ctx")
    chips = n // 2
    chip, c = me // 2, me % 2
    heads, nope_w, lat_w = kup_v.shape
    value_w = vup_hbm.shape[2]
    rows = x_v.shape[0]
    requests, keys, _ = lat_hbm.shape
    chip_keys = 2 * keys
    model = out_ref.shape[1]
    half = model // 2
    stretch = rows // requests
    block_rows = heads * stretch
    rope_w = ropew_v.shape[1] // heads
    q_w = qbuf.shape[3]
    hv_w = heads * value_w
    owners = opart.shape[1]
    base = (chips - owners) // 2
    width = opart.shape[3]
    scale = mscale_yarn * mscale_yarn / math.sqrt(nope_w + rope_w)
    scale2 = scale * math.log2(math.e)
    partner = chip * 2 + 1 - c

    def peer(k):
        flipped, bit = 0, 1
        while bit < chips:
            flipped = flipped + ((chip // bit + (k // bit) % 2) % 2) * bit
            bit *= 2
        return flipped

    near_first = sorted(range(1, chips), key=lambda k: (bin(k).count("1"), k))
    far_first = near_first[::-1]

    def remote(src, dst, ssem, rsem, target):
        return pltpu.make_async_remote_copy(
            src_ref=src, dst_ref=dst, send_sem=ssem, recv_sem=rsem,
            device_id={"ctx": target}, device_id_type=MESH,
        )

    loads = []

    def load(src, dst):
        copy = pltpu.make_async_copy(src, dst, ld_sem.at[len(loads)])
        copy.start()
        loads.append(copy)
        return copy

    barrier = pltpu.get_barrier_semaphore()
    load_x = load(x_hbm, x_v)
    load_gain = load(gain_hbm, gain_v)
    load_nope = load(nope_hbm, nope_v)
    load_rope = load(ropew_hbm, ropew_v)
    load_kup = load(kup_hbm, kup_v)
    load_len = load(len_hbm, len_s)
    for k in far_first:
        pl.semaphore_signal(
            barrier, inc=1, device_id={"ctx": peer(k) * 2 + c}, device_id_type=MESH
        )
    pl.semaphore_signal(barrier, inc=1, device_id={"ctx": partner}, device_id_type=MESH)

    load_x.wait()
    load_gain.wait()
    widened = x_v[...].astype(F32)
    normed = (
        widened
        * lax.rsqrt(jnp.mean(widened * widened, axis=-1, keepdims=True) + 1e-06)
        * gain_v[...].astype(F32).reshape(1, -1)
    ).astype(BF16)
    load_nope.wait()
    query_nope = jnp.dot(normed, nope_v[...], preferred_element_type=F32).astype(BF16)
    load_rope.wait()
    query_rope = jnp.dot(normed, ropew_v[...], preferred_element_type=F32)
    load_kup.wait()

    mine = lambda at: pl.ds(pl.multiple_of(at * keys, 128), keys)
    out_rows = outw_hbm.shape[0]
    columns = lambda at: pl.ds(pl.multiple_of(at * half, 128), half)
    load_cache = []
    for b in range(requests):
        load_cache.append([
            load(lat_hbm.at[b], lat_v.at[b, mine(c)]),
            load(crope_hbm.at[b], crope_v.at[b, :, mine(c)]),
        ])
    load_late = [
        load(vup_hbm.at[h], vup_v.at[:, h * value_w : (h + 1) * value_w]) for h in range(heads)
    ]
    w_rows = lambda at: pl.ds(pl.multiple_of(at * out_rows, out_rows), out_rows)
    load_late.append(load(outw_hbm.at[:, columns(c)], outw_v.at[w_rows(c), :half]))
    if outw_v.shape[1] > half:
        outw_v[:, half:] = jnp.zeros((outw_v.shape[0], outw_v.shape[1] - half), BF16)

    latents = [
        jnp.dot(
            query_nope[:, h * nope_w : (h + 1) * nope_w], kup_v[h], preferred_element_type=F32
        )
        for h in range(heads)
    ]
    for b in range(requests):
        part = slice(b * stretch, (b + 1) * stretch)
        qbuf[b, chip, :, :lat_w] = jnp.concatenate([t[part] for t in latents], axis=0).astype(BF16)
    qbuf[0, chip, :, lat_w:] = jnp.concatenate(
        [
            jnp.concatenate(
                [
                    query_rope[b * stretch : (b + 1) * stretch, h * rope_w : (h + 1) * rope_w]
                    for b in range(requests)
                ],
                axis=1,
            )
            for h in range(heads)
        ],
        axis=0,
    ).astype(BF16)
    pl.semaphore_wait(barrier, chips)

    pending = []

    def send(copy):
        copy.start()
        pending.append(copy)

    def query_copy(b, source, k, target):
        ref = qbuf.at[b, source] if b == 0 else qbuf.at[b, source, :, :lat_w]
        return remote(ref, ref, qs.at[b, k], qr.at[b, k], target)

    def kv_copies(b, side):
        return [
            remote(lat_hbm.at[b], lat_v.at[b, mine(side)], kvs.at[b, 0], kvr.at[b, 0], partner),
            remote(
                crope_hbm.at[b], crope_v.at[b, :, mine(side)], kvs.at[b, 1], kvr.at[b, 1], partner
            ),
        ]

    def w_copy(side):
        return remote(
            outw_hbm.at[:, columns(1 - c)], outw_v.at[w_rows(side), :half],
            kvs.at[requests, 0], kvr.at[requests, 0], partner,
        )

    for b in range(requests):
        for k in far_first:
            send(query_copy(b, chip, k, peer(k) * 2 + c))
    for b in range(requests):
        for copy in kv_copies(b, c):
            send(copy)
    send(w_copy(c))

    load_len.wait()
    first_key = chip * chip_keys
    per_request = chips * block_rows
    tiles = per_request // tile
    tile_chips = tile // block_rows
    lane = lax.broadcasted_iota(jnp.int32, (tile, 128), 1)

    def attend(b, d0):
        query = qbuf[b, pl.ds(d0, tile_chips), :, :lat_w].reshape(tile, lat_w)
        rope_at = lat_w + b * rope_w
        rope = qbuf[0, pl.ds(d0, tile_chips), :, rope_at : rope_at + rope_w].reshape(tile, rope_w)
        row = lax.broadcasted_iota(jnp.int32, (tile, 1), 0) % stretch
        limit = len_s[b] + row - first_key
        peak = None
        for at in range(0, chip_keys, chunk):
            span = slice(at, at + chunk)
            raw = lax.dot_general(query, lat_v[b, span], NT, preferred_element_type=F32)
            raw = raw + jnp.dot(rope, crope_v[b, :, span], preferred_element_type=F32)
            where_key = lax.broadcasted_iota(jnp.int32, (tile, chunk), 1) + at
            raw = jnp.where(where_key <= limit, raw, masked_score)
            score_s[:, span] = raw
            high = jnp.max(raw, axis=1, keepdims=True)
            peak = high if peak is None else jnp.maximum(peak, high)
        total, pooled = None, None
        for at in range(0, chip_keys, chunk):
            span = slice(at, at + chunk)
            weights = jnp.exp2((score_s[:, span] - peak) * scale2)
            part = jnp.sum(weights, axis=1, keepdims=True)
            pool = jnp.dot(weights.astype(BF16), lat_v[b, span], preferred_element_type=F32)
            total = part if total is None else total + part
            pooled = pool if pooled is None else pooled + pool
        peak = jnp.broadcast_to(peak, (tile, 128))
        total = jnp.broadcast_to(total, (tile, 128))
        stat = jnp.zeros((tile, 128), F32)
        for i, piece in enumerate(pieces(peak) + pieces(total)):
            stat = jnp.where(lane == i, piece, stat)
        to = pl.ds(d0, tile_chips)
        sb[b, to, :, :lat_w] = pooled.astype(BF16).reshape(tile_chips, block_rows, lat_w)
        sb[b, to, :, lat_w:] = stat.astype(BF16).reshape(tile_chips, block_rows, 128)
        pool_s[b, to] = pooled.reshape(tile_chips, block_rows, lat_w)
        stat_s[b, to] = jnp.where(lane < 64, peak, total).reshape(tile_chips, block_rows, 128)

    def pool_copy(b, k, slot):
        return remote(
            sb.at[b, peer(k)], rb.at[b, slot], ps.at[b, k], pr.at[b, k], peer(k) * 2 + c
        )

    for b in range(requests):
        for copy in load_cache[b]:
            copy.wait()
        for k in near_first:
            query_copy(b, peer(k), k, peer(k) * 2 + c).wait_recv()
        for copy in kv_copies(b, 1 - c):
            copy.wait_recv()
        if tiles == 1:
            attend(b, 0)
        else:
            def step(t, carry, b=b):
                attend(b, t * tile_chips)
                return carry
            lax.fori_loop(0, tiles, step, 0)
        for k in far_first:
            send(pool_copy(b, k, chip))

    def hv_copy(b, side):
        return remote(hvbuf.at[b, side], hvbuf.at[b, side], hs.at[b], hr.at[b], partner)

    def combine(b):
        own = stat_s[b, chip]
        parts = [(own[:, 0:1], own[:, 64:65], pool_s[b, chip])]
        for k in near_first:
            pool_copy(b, k, peer(k)).wait_recv()
        for k in near_first:
            stat = rb[b, peer(k), :, lat_w:].astype(F32)
            peak = stat[:, 0:1] + stat[:, 1:2] + stat[:, 2:3]
            total = stat[:, 3:4] + stat[:, 4:5] + stat[:, 5:6]
            parts.append((peak, total, rb[b, peer(k), :, :lat_w].astype(F32)))
        top = functools.reduce(jnp.maximum, [peak for peak, _, _ in parts])
        sums, pooled = 0.0, 0.0
        for peak, total, pool in parts:
            factor = jnp.exp2((peak - top) * scale2)
            sums = sums + factor * total
            pooled = pooled + factor * pool
        attended = (pooled / sums).astype(BF16)
        values = jnp.dot(attended, vup_v[...], preferred_element_type=F32)
        hvbuf[b, c] = jnp.concatenate(
            [
                values[h * stretch : (h + 1) * stretch, h * value_w : (h + 1) * value_w]
                for h in range(heads)
            ],
            axis=1,
        ).astype(BF16)
        send(hv_copy(b, c))

    upper = chip // (chips // 2)

    def far_owner(i):
        return (owners - 1 - i) * (1 - upper) + i * upper

    def out_copy(b, o):
        return remote(
            ob.at[b, o], orb.at[b, chip], os.at[b, o], orr.at[b, chip], (base + o) * 2 + c
        )

    def project(b):
        hv_copy(b, 1 - c).wait_recv()
        head_values = jnp.concatenate([hvbuf[b, 0], hvbuf[b, 1]], axis=1)
        for i in range(owners):
            o = far_owner(i)
            at = pl.ds(pl.multiple_of(o * width, 128), width)
            piece = jnp.dot(head_values, outw_v[:, at], preferred_element_type=F32)
            opart[b, o] = piece
            ob[b, o] = piece.astype(BF16)

            @pl.when(chip != base + o)
            def _():
                out_copy(b, o).start()

    is_owner = jnp.logical_and(chip >= base, chip < base + owners)

    def fin_copy(b, o, k):
        return remote(
            fin.at[b, c, o], fin.at[b, c, o], fs.at[b, k], fr.at[b, o], peer(k) * 2 + c
        )

    def relay_copy(b, side, o):
        ref = fin.at[b, side, o]
        return remote(ref, ref, gs.at[b, o], gr.at[b, o], partner)

    def reduce_out(b):
        @pl.when(is_owner)
        def _():
            o = chip - base
            summed = opart[b, o]
            for k in near_first:
                remote(
                    ob.at[b, 0], orb.at[b, peer(k)], os.at[b, 0], orr.at[b, peer(k)],
                    peer(k) * 2 + c,
                ).wait_recv()
            for k in near_first:
                summed = summed + orb[b, peer(k)].astype(F32)
            fin[b, c, o] = summed.astype(BF16)
            for k in far_first:
                fin_copy(b, o, k).start()

    def spread(b):
        for i in reversed(range(owners)):
            o = far_owner(i)

            @pl.when(chip != base + o)
            def _():
                fin_copy(b, o, 1).wait_recv()

            send(relay_copy(b, c, o))

    for copy in load_late:
        copy.wait()
    for b in range(requests):
        combine(b)
        if b == 0:
            w_copy(1 - c).wait_recv()
        project(b)
    for b in range(requests):
        reduce_out(b)
    for b in range(requests):
        spread(b)
    for b in range(requests):
        for i in reversed(range(owners)):
            relay_copy(b, 1 - c, far_owner(i)).wait_recv()

    for side in range(2):
        for o in range(owners):
            used = max(0, min(width, half - o * width))
            if used:
                at = side * half + o * width
                out_ref[:, at : at + used] = jnp.concatenate(
                    [fin[b, side, o, :, :used].astype(F32) for b in range(requests)], axis=0
                ).astype(BF16)
    for copy in pending:
        copy.wait_send()
    for b in range(requests):
        for o in range(owners):
            @pl.when(chip != base + o)
            def _():
                out_copy(b, o).wait_send()

        @pl.when(is_owner)
        def _():
            for k in far_first:
                fin_copy(b, chip - base, k).wait_send()


def local(
    n, query_input, query_gain, nope_weight, rope_weight, key_up, value_up, out_weight,
    cache_latent, cache_rope, cached_length,
):
    heads, _, lat_w = key_up.shape
    value_w = value_up.shape[2]
    rows = query_input.shape[0]
    requests, keys, _ = cache_latent.shape
    rope_w = rope_weight.shape[1] // heads
    stretch = rows // requests
    block_rows = heads * stretch
    model = out_weight.shape[1]
    half = model // 2
    chips = n // 2
    owners = max(1, chips // 2)
    tile = min(128, chips * block_rows)
    chunk = min(1024, 2 * keys)
    width = -(-half // (128 * owners)) * 128
    vmem = pltpu.VMEM
    dma = lambda *count: pltpu.SemaphoreType.DMA(count)
    any_spec = pl.BlockSpec(memory_space=pl.ANY)
    per_block = (requests, chips, block_rows)
    pair = lambda count: [dma(requests, count)] * 2
    return pl.pallas_call(
        functools.partial(kernel, n, tile, chunk),
        out_shape=jax.ShapeDtypeStruct((rows, model), BF16),
        in_specs=[any_spec] * 10,
        out_specs=pl.BlockSpec(memory_space=pltpu.VMEM),
        scratch_shapes=[
            vmem(query_input.shape, BF16), vmem(query_gain.shape, BF16),
            vmem(nope_weight.shape, BF16), vmem(rope_weight.shape, BF16),
            vmem(key_up.shape, BF16), vmem((lat_w, heads * value_w), BF16),
            vmem((2 * out_weight.shape[0], owners * width), BF16),
            vmem((requests, 2 * keys, lat_w), BF16),
            vmem((requests, rope_w, 2 * keys), BF16),
            pltpu.SMEM(cached_length.shape, jnp.int32),
            vmem((*per_block, lat_w + requests * rope_w), BF16),
            vmem((tile, 2 * keys), F32),
            vmem((*per_block, 128), F32), vmem((*per_block, lat_w), F32),
            vmem((*per_block, lat_w + 128), BF16), vmem((*per_block, lat_w + 128), BF16),
            vmem((requests, 2, stretch, heads * value_w), BF16),
            vmem((requests, owners, stretch, width), F32),
            vmem((requests, owners, stretch, width), BF16),
            vmem((requests, chips, stretch, width), BF16),
            vmem((requests, 2, owners, stretch, width), BF16),
            dma(6 + 2 * requests + heads + 1),
            dma(requests + 1, 2), dma(requests + 1, 2),
            *pair(chips), *pair(chips), dma(requests), dma(requests),
            dma(requests, owners), dma(requests, chips),
            dma(requests, chips), dma(requests, owners), *pair(owners),
        ],
        compiler_params=pltpu.CompilerParams(
            collective_id=0, has_side_effects=True, vmem_limit_bytes=63 * 1024 * 1024
        ),
    )(
        query_input, query_gain, nope_weight, rope_weight, key_up,
        value_up, out_weight, cache_latent, cache_rope, cached_length,
    )


def solution(mesh):
    placed = (
        P("groups", None),
        P(),
        P(None, "ctx"),
        P(None, "ctx"),
        P("ctx", None, None),
        P("ctx", None, None),
        P("ctx", None),
        P("groups", "ctx", None),
        P("groups", None, "ctx"),
        P("groups"),
    )
    return jax.shard_map(
        functools.partial(local, mesh.shape["ctx"]), mesh=mesh, in_specs=placed,
        out_specs=P("groups", None), check_vma=False,
    )
```

```python
import functools
import math

import jax
import jax.numpy as jnp
from jax import lax
from jax.experimental import pallas as pl
from jax.experimental.pallas import tpu as pltpu
from jax.sharding import PartitionSpec as P

mscale_yarn = 1.0 + 0.1 * math.log(40.0)
masked_score = -1e30
MESH = pl.DeviceIdType.MESH
F32 = jnp.float32
BF16 = jnp.bfloat16
NT = (((1,), (1,)), ((), ()))


def pieces(value):
    out = []
    for _ in range(3):
        piece = value.astype(BF16).astype(F32)
        out.append(piece)
        value = value - piece
    return out


def kernel(
    n, tile, chunk,
    x_hbm, gain_hbm, nope_hbm, ropew_hbm, kup_hbm, vup_hbm, outw_hbm, lat_hbm, crope_hbm, len_hbm,
    out_ref,
    x_v, gain_v, nope_v, ropew_v, kup_v, vup_v, outw_v, lat_v, crope_v, len_s,
    qbuf, score_s, stat_s, pool_s, sb, rb, hvbuf, opart, ob, orb, fin,
    ld_sem, kvs, kvr, qs, qr, pr, hr, os, orr, fs, fr, gs, gr,
):
    me = lax.axis_index("ctx")
    chips = n // 2
    chip, c = me // 2, me % 2
    heads, nope_w, lat_w = kup_v.shape
    value_w = vup_hbm.shape[2]
    rows = x_v.shape[0]
    requests, keys, _ = lat_hbm.shape
    chip_keys = 2 * keys
    model = out_ref.shape[1]
    half = model // 2
    stretch = rows // requests
    block_rows = heads * stretch
    rope_w = ropew_v.shape[1] // heads
    q_w = qbuf.shape[3]
    hv_w = heads * value_w
    owners = opart.shape[1]
    base = (chips - owners) // 2
    width = opart.shape[3]
    scale = mscale_yarn * mscale_yarn / math.sqrt(nope_w + rope_w)
    scale2 = scale * math.log2(math.e)
    partner = chip * 2 + 1 - c

    def peer(k):
        flipped, bit = 0, 1
        while bit < chips:
            flipped = flipped + ((chip // bit + (k // bit) % 2) % 2) * bit
            bit *= 2
        return flipped

    near_first = sorted(range(1, chips), key=lambda k: (bin(k).count("1"), k))
    far_first = near_first[::-1]

    def remote(src, dst, ssem, rsem, target):
        return pltpu.make_async_remote_copy(
            src_ref=src, dst_ref=dst, send_sem=ssem, recv_sem=rsem,
            device_id={"ctx": target}, device_id_type=MESH,
        )

    def load(src, dst, slot):
        copy = pltpu.make_async_copy(src, dst, ld_sem.at[slot])
        copy.start()
        return copy

    barrier = pltpu.get_barrier_semaphore()
    load_x = load(x_hbm, x_v, 0)
    load_gain = load(gain_hbm, gain_v, 1)
    load_nope = load(nope_hbm, nope_v, 2)
    load_rope = load(ropew_hbm, ropew_v, 3)
    load_kup = load(kup_hbm, kup_v, 4)
    load_len = load(len_hbm, len_s, 5)
    for k in far_first:
        pl.semaphore_signal(
            barrier, inc=1, device_id={"ctx": peer(k) * 2 + c}, device_id_type=MESH
        )
    pl.semaphore_signal(barrier, inc=1, device_id={"ctx": partner}, device_id_type=MESH)

    load_x.wait()
    load_gain.wait()
    widened = x_v[...].astype(F32)
    normed = (
        widened
        * lax.rsqrt(jnp.mean(widened * widened, axis=-1, keepdims=True) + 1e-06)
        * gain_v[...].astype(F32).reshape(1, -1)
    ).astype(BF16)
    load_nope.wait()
    query_nope = jnp.dot(normed, nope_v[...], preferred_element_type=F32).astype(BF16)
    load_rope.wait()
    query_rope = jnp.dot(normed, ropew_v[...], preferred_element_type=F32)
    load_kup.wait()
    load_len.wait()

    mine = lambda at: pl.ds(pl.multiple_of(at * keys, 128), keys)
    out_rows = outw_hbm.shape[0]
    columns = lambda at: pl.ds(pl.multiple_of(at * half, 128), half)
    w_rows = lambda at: pl.ds(pl.multiple_of(at * out_rows, out_rows), out_rows)
    load_crope = load(crope_hbm, crope_v.at[:, :, mine(c)], 0)
    load_lat = [load(lat_hbm.at[b], lat_v.at[b, mine(c)], 1 + b) for b in range(requests)]
    load_late = [
        load(vup_hbm.at[h], vup_v.at[:, h * value_w : (h + 1) * value_w], 1 + requests + h)
        for h in range(heads)
    ]
    load_late.append(
        load(outw_hbm.at[:, columns(c)], outw_v.at[w_rows(c), :half], 1 + requests + heads)
    )
    if outw_v.shape[1] > half:
        outw_v[:, half:] = jnp.zeros((outw_v.shape[0], outw_v.shape[1] - half), BF16)

    latents = [
        jnp.dot(
            query_nope[:, h * nope_w : (h + 1) * nope_w], kup_v[h], preferred_element_type=F32
        )
        for h in range(heads)
    ]
    for b in range(requests):
        part = slice(b * stretch, (b + 1) * stretch)
        qbuf[b, chip, :, :lat_w] = jnp.concatenate([t[part] for t in latents], axis=0).astype(BF16)
    qbuf[0, chip, :, lat_w:] = jnp.concatenate(
        [
            jnp.concatenate(
                [
                    query_rope[b * stretch : (b + 1) * stretch, h * rope_w : (h + 1) * rope_w]
                    for b in range(requests)
                ],
                axis=1,
            )
            for h in range(heads)
        ],
        axis=0,
    ).astype(BF16)
    pl.semaphore_wait(barrier, chips)

    others = pl.ds(0, chips - 1)

    def sent(ref, sem):
        remote(ref, ref, sem, sem, partner).wait_send()

    def received(ref, sem):
        remote(ref, ref, sem, sem, partner).wait_recv()

    def queries(b, at):
        return qbuf.at[b, at] if b == 0 else qbuf.at[b, at, :, :lat_w]

    def lat_copy(b, side):
        return remote(lat_hbm.at[b], lat_v.at[b, mine(side)], kvs.at[b], kvr.at[b], partner)

    def crope_copy(side):
        return remote(
            crope_hbm, crope_v.at[:, :, mine(side)], kvs.at[requests], kvr.at[requests], partner
        )

    def w_copy(side):
        return remote(
            outw_hbm.at[:, columns(1 - c)], outw_v.at[w_rows(side), :half],
            kvs.at[requests + 1], kvr.at[requests + 1], partner,
        )

    def send_queries(b, ks):
        for k in ks:
            ref = queries(b, chip)
            remote(ref, ref, qs.at[b], qr.at[b], peer(k) * 2 + c).start()

    send_queries(0, far_first)
    crope_copy(c).start()
    for b in range(requests):
        lat_copy(b, c).start()
    received(queries(0, others), qr.at[0])
    for b in range(1, requests):
        send_queries(b, far_first)
    first_key = chip * chip_keys
    per_request = chips * block_rows
    tiles = per_request // tile
    tile_chips = tile // block_rows
    lane = lax.broadcasted_iota(jnp.int32, (tile, 128), 1)

    def attend(b, d0):
        query = qbuf[b, pl.ds(d0, tile_chips), :, :lat_w].reshape(tile, lat_w)
        rope_at = lat_w + b * rope_w
        rope = qbuf[0, pl.ds(d0, tile_chips), :, rope_at : rope_at + rope_w].reshape(tile, rope_w)
        row = lax.broadcasted_iota(jnp.int32, (tile, 1), 0) % stretch
        limit = len_s[b] + row - first_key
        peak = None
        for at in range(0, chip_keys, chunk):
            span = slice(at, at + chunk)
            raw = lax.dot_general(query, lat_v[b, span], NT, preferred_element_type=F32)
            raw = raw + jnp.dot(rope, crope_v[b, :, span], preferred_element_type=F32)
            where_key = lax.broadcasted_iota(jnp.int32, (tile, chunk), 1) + at
            raw = jnp.where(where_key <= limit, raw, masked_score)
            score_s[:, span] = raw
            high = jnp.max(raw, axis=1, keepdims=True)
            peak = high if peak is None else jnp.maximum(peak, high)
        total, pooled = None, None
        for at in range(0, chip_keys, chunk):
            span = slice(at, at + chunk)
            weights = jnp.exp2((score_s[:, span] - peak) * scale2)
            part = jnp.sum(weights, axis=1, keepdims=True)
            pool = jnp.dot(weights.astype(BF16), lat_v[b, span], preferred_element_type=F32)
            total = part if total is None else total + part
            pooled = pool if pooled is None else pooled + pool
        peak = jnp.broadcast_to(peak, (tile, 128))
        total = jnp.broadcast_to(total, (tile, 128))
        stat = jnp.zeros((tile, 128), F32)
        for i, piece in enumerate(pieces(peak) + pieces(total)):
            stat = jnp.where(lane == i, piece, stat)
        to = pl.ds(d0, tile_chips)
        sb[b, to, :, :lat_w] = pooled.astype(BF16).reshape(tile_chips, block_rows, lat_w)
        sb[b, to, :, lat_w:] = stat.astype(BF16).reshape(tile_chips, block_rows, 128)
        pool_s[b, to] = pooled.reshape(tile_chips, block_rows, lat_w)
        stat_s[b, to] = jnp.where(lane < 64, peak, total).reshape(tile_chips, block_rows, 128)

    for b in range(requests):
        load_lat[b].wait()
        if b == 0:
            load_crope.wait()
        if b:
            received(queries(b, others), qr.at[b])
        if b == 0:
            crope_copy(1 - c).wait_recv()
        lat_copy(b, 1 - c).wait_recv()
        if tiles == 1:
            attend(b, 0)
        else:
            def step(t, carry, b=b):
                attend(b, t * tile_chips)
                return carry
            lax.fori_loop(0, tiles, step, 0)
        sent(queries(b, others), qs.at[b])
        for k in far_first:
            remote(
                sb.at[b, peer(k)], rb.at[b, chip], qs.at[b], pr.at[b], peer(k) * 2 + c
            ).start()
        if b == 0:
            w_copy(c).start()

    def hv_copy(b, side):
        return remote(hvbuf.at[b, side], hvbuf.at[b, side], qs.at[b], hr.at[b], partner)

    def combine(b):
        own = stat_s[b, chip]
        parts = [(own[:, 0:1], own[:, 64:65], pool_s[b, chip])]
        received(rb.at[b, others], pr.at[b])
        for k in near_first:
            stat = rb[b, peer(k), :, lat_w:].astype(F32)
            peak = stat[:, 0:1] + stat[:, 1:2] + stat[:, 2:3]
            total = stat[:, 3:4] + stat[:, 4:5] + stat[:, 5:6]
            parts.append((peak, total, rb[b, peer(k), :, :lat_w].astype(F32)))
        top = functools.reduce(jnp.maximum, [peak for peak, _, _ in parts])
        sums, pooled = 0.0, 0.0
        for peak, total, pool in parts:
            factor = jnp.exp2((peak - top) * scale2)
            sums = sums + factor * total
            pooled = pooled + factor * pool
        attended = (pooled / sums).astype(BF16)
        values = jnp.dot(attended, vup_v[...], preferred_element_type=F32)
        hvbuf[b, c] = jnp.concatenate(
            [
                values[h * stretch : (h + 1) * stretch, h * value_w : (h + 1) * value_w]
                for h in range(heads)
            ],
            axis=1,
        ).astype(BF16)
        sent(sb.at[b, others], qs.at[b])
        hv_copy(b, c).start()

    upper = chip // (chips // 2)

    def far_owner(i):
        return (owners - 1 - i) * (1 - upper) + i * upper

    def out_copy(b, o):
        return remote(
            ob.at[b, o], orb.at[b, chip], os.at[b], orr.at[b], (base + o) * 2 + c
        )

    def project(b):
        hv_copy(b, 1 - c).wait_recv()
        head_values = jnp.concatenate([hvbuf[b, 0], hvbuf[b, 1]], axis=1)
        for i in range(owners):
            o = far_owner(i)
            at = pl.ds(pl.multiple_of(o * width, 128), width)
            piece = jnp.dot(head_values, outw_v[:, at], preferred_element_type=F32)
            opart[b, o] = piece
            ob[b, o] = piece.astype(BF16)

            @pl.when(chip != base + o)
            def _():
                out_copy(b, o).start()

    is_owner = jnp.logical_and(chip >= base, chip < base + owners)

    def fin_copy(b, o, k):
        ref = fin.at[b, c, o]
        return remote(ref, ref, fs.at[b], fr.at[b], peer(k) * 2 + c)

    def relay_copy(b, side):
        ref = fin.at[b, side]
        return remote(ref, ref, gs.at[b], gr.at[b], partner)

    def reduce_out(b):
        @pl.when(is_owner)
        def _():
            o = chip - base
            received(orb.at[b, others], orr.at[b])
            summed = opart[b, o]
            for k in near_first:
                summed = summed + orb[b, peer(k)].astype(F32)
            fin[b, c, o] = summed.astype(BF16)
            for k in far_first:
                fin_copy(b, o, k).start()

    def by_role(wait):
        if owners > 1:
            @pl.when(is_owner)
            def _():
                wait(pl.ds(0, owners - 1))

        @pl.when(jnp.logical_not(is_owner))
        def _():
            wait(pl.ds(0, owners))

    def place(side):
        for core in range(2):
            @pl.when(side == core)
            def _():
                for o in range(owners):
                    used = min(width, half - o * width)
                    if used > 0:
                        at = core * half + o * width
                        out_ref[:, at : at + used] = jnp.concatenate(
                            [fin[b, core, o, :, :used].astype(F32) for b in range(requests)],
                            axis=0,
                        ).astype(BF16)

    for copy in load_late:
        copy.wait()
    for b in range(requests):
        combine(b)
        if b == 0:
            w_copy(1 - c).wait_recv()
        project(b)
    for b in range(requests):
        reduce_out(b)
    crope_copy(c).wait_send()
    for b in range(requests):
        lat_copy(b, c).wait_send()
        sent(hvbuf.at[b, c], qs.at[b])
        by_role(lambda part: sent(ob.at[b, part], os.at[b]))
    w_copy(c).wait_send()
    for b in range(requests):
        by_role(lambda part: received(fin.at[b, c, part], fr.at[b]))
        relay_copy(b, c).start()
    place(c)

    @pl.when(is_owner)
    def _():
        for b in range(requests):
            sent(orb.at[b, others], fs.at[b])

    for b in range(requests):
        relay_copy(b, 1 - c).wait_recv()
    place(1 - c)
    for b in range(requests):
        relay_copy(b, c).wait_send()


def local(
    n, query_input, query_gain, nope_weight, rope_weight, key_up, value_up, out_weight,
    cache_latent, cache_rope, cached_length,
):
    heads, _, lat_w = key_up.shape
    value_w = value_up.shape[2]
    rows = query_input.shape[0]
    requests, keys, _ = cache_latent.shape
    rope_w = rope_weight.shape[1] // heads
    stretch = rows // requests
    block_rows = heads * stretch
    model = out_weight.shape[1]
    half = model // 2
    chips = n // 2
    owners = max(1, chips // 2)
    tile = min(128, chips * block_rows)
    chunk = min(1024, 2 * keys)
    width = -(-half // (128 * owners)) * 128
    vmem = pltpu.VMEM
    dma = lambda *count: pltpu.SemaphoreType.DMA(count)
    any_spec = pl.BlockSpec(memory_space=pl.ANY)
    per_block = (requests, chips, block_rows)
    return pl.pallas_call(
        functools.partial(kernel, n, tile, chunk),
        out_shape=jax.ShapeDtypeStruct((rows, model), BF16),
        in_specs=[any_spec] * 10,
        out_specs=pl.BlockSpec(memory_space=pltpu.VMEM),
        scratch_shapes=[
            vmem(query_input.shape, BF16), vmem(query_gain.shape, BF16),
            vmem(nope_weight.shape, BF16), vmem(rope_weight.shape, BF16),
            vmem(key_up.shape, BF16), vmem((lat_w, heads * value_w), BF16),
            vmem((2 * out_weight.shape[0], owners * width), BF16),
            vmem((requests, 2 * keys, lat_w), BF16),
            vmem((requests, rope_w, 2 * keys), BF16),
            pltpu.SMEM(cached_length.shape, jnp.int32),
            vmem((*per_block, lat_w + requests * rope_w), BF16),
            vmem((tile, 2 * keys), F32),
            vmem((*per_block, 128), F32), vmem((*per_block, lat_w), F32),
            vmem((*per_block, lat_w + 128), BF16), vmem((*per_block, lat_w + 128), BF16),
            vmem((requests, 2, stretch, heads * value_w), BF16),
            vmem((requests, owners, stretch, width), F32),
            vmem((requests, owners, stretch, width), BF16),
            vmem((requests, chips, stretch, width), BF16),
            vmem((requests, 2, owners, stretch, width), BF16),
            dma(max(6, 2 + requests + heads)), dma(requests + 2), dma(requests + 2),
            *[dma(requests)] * 10,
        ],
        compiler_params=pltpu.CompilerParams(
            collective_id=0, has_side_effects=True, vmem_limit_bytes=40 * 1024 * 1024
        ),
    )(*[
        pltpu.with_memory_space_constraint(array, pltpu.HBM)
        for array in (
            query_input, query_gain, nope_weight, rope_weight, key_up,
            value_up, out_weight, cache_latent, cache_rope, cached_length,
        )
    ])


def solution(mesh):
    placed = (
        P("groups", None),
        P(),
        P(None, "ctx"),
        P(None, "ctx"),
        P("ctx", None, None),
        P("ctx", None, None),
        P("ctx", None),
        P("groups", "ctx", None),
        P("groups", None, "ctx"),
        P("groups"),
    )
    return jax.shard_map(
        functools.partial(local, mesh.shape["ctx"]), mesh=mesh, in_specs=placed,
        out_specs=P("groups", None), check_vma=False,
    )
```

```python
import functools
import math

import jax
import jax.numpy as jnp
from jax import lax
from jax.experimental import pallas as pl
from jax.experimental.pallas import tpu as pltpu
from jax.sharding import PartitionSpec as P

mscale_yarn = 1.0 + 0.1 * math.log(40.0)
masked_score = -1e30
MESH = pl.DeviceIdType.MESH
F32 = jnp.float32
BF16 = jnp.bfloat16
NT = (((1,), (1,)), ((), ()))


def kernel(
    n, tile, chunk,
    x_hbm, gain_hbm, nope_hbm, ropew_hbm, kup_hbm, vup_hbm, outw_hbm, lat_hbm, crope_hbm, len_hbm,
    out_ref,
    x_v, gain_v, nope_v, ropew_v, kup_v, vup_v, outw_v, lat_v, crope_v, len_s,
    qbuf, score_s, stat_b, turn_s, pool_s, sb, rb, hvbuf, opart, ob, orb, fin,
    ld_sem, kvs, kvr, qs, qr, ts, tr, pr, hr, os, orr, fs, fr, gs, gr,
):
    me = lax.axis_index("ctx")
    chips = n // 2
    chip, c = me // 2, me % 2
    heads, nope_w, lat_w = kup_v.shape
    value_w = vup_hbm.shape[2]
    rows = x_v.shape[0]
    requests, keys, _ = lat_hbm.shape
    chip_keys = 2 * keys
    model = out_ref.shape[1]
    half = model // 2
    stretch = rows // requests
    block_rows = heads * stretch
    rope_w = ropew_v.shape[1] // heads
    q_w = qbuf.shape[3]
    hv_w = heads * value_w
    owners = opart.shape[1]
    base = (chips - owners) // 2
    width = opart.shape[3]
    scale = mscale_yarn * mscale_yarn / math.sqrt(nope_w + rope_w)
    scale2 = scale * math.log2(math.e)
    partner = chip * 2 + 1 - c

    def peer(k):
        flipped, bit = 0, 1
        while bit < chips:
            flipped = flipped + ((chip // bit + (k // bit) % 2) % 2) * bit
            bit *= 2
        return flipped

    near_first = sorted(range(1, chips), key=lambda k: (bin(k).count("1"), k))
    far_first = near_first[::-1]

    def remote(src, dst, ssem, rsem, target):
        return pltpu.make_async_remote_copy(
            src_ref=src, dst_ref=dst, send_sem=ssem, recv_sem=rsem,
            device_id={"ctx": target}, device_id_type=MESH,
        )

    def load(src, dst, slot):
        copy = pltpu.make_async_copy(src, dst, ld_sem.at[slot])
        copy.start()
        return copy

    barrier = pltpu.get_barrier_semaphore()
    load_x = load(x_hbm, x_v, 0)
    load_gain = load(gain_hbm, gain_v, 1)
    load_nope = load(nope_hbm, nope_v, 2)
    load_rope = load(ropew_hbm, ropew_v, 3)
    load_kup = load(kup_hbm, kup_v, 4)
    load_len = load(len_hbm, len_s, 5)
    for k in far_first:
        pl.semaphore_signal(
            barrier, inc=1, device_id={"ctx": peer(k) * 2 + c}, device_id_type=MESH
        )
    pl.semaphore_signal(barrier, inc=1, device_id={"ctx": partner}, device_id_type=MESH)

    load_x.wait()
    load_gain.wait()
    widened = x_v[...].astype(F32)
    normed = (
        widened
        * lax.rsqrt(jnp.mean(widened * widened, axis=-1, keepdims=True) + 1e-06)
        * gain_v[...].astype(F32).reshape(1, -1)
    ).astype(BF16)
    load_nope.wait()
    load_rope.wait()
    load_kup.wait()
    load_len.wait()
    query_nope = jnp.dot(normed, nope_v[...], preferred_element_type=F32).astype(BF16)
    query_rope = jnp.dot(normed, ropew_v[...], preferred_element_type=F32)

    latents = [
        jnp.dot(
            query_nope[:, h * nope_w : (h + 1) * nope_w], kup_v[h], preferred_element_type=F32
        )
        for h in range(heads)
    ]
    for b in range(requests):
        part = slice(b * stretch, (b + 1) * stretch)
        qbuf[b, chip, :, :lat_w] = jnp.concatenate([t[part] for t in latents], axis=0).astype(BF16)
    qbuf[0, chip, :, lat_w:] = jnp.concatenate(
        [
            jnp.concatenate(
                [
                    query_rope[b * stretch : (b + 1) * stretch, h * rope_w : (h + 1) * rope_w]
                    for b in range(requests)
                ],
                axis=1,
            )
            for h in range(heads)
        ],
        axis=0,
    ).astype(BF16)
    mine = lambda at: pl.ds(pl.multiple_of(at * keys, 128), keys)
    out_rows = outw_hbm.shape[0]
    columns = lambda at: pl.ds(pl.multiple_of(at * half, 128), half)
    w_rows = lambda at: pl.ds(pl.multiple_of(at * out_rows, out_rows), out_rows)
    load_crope = load(crope_hbm, crope_v.at[:, :, mine(c)], 0)
    load_lat = [load(lat_hbm.at[b], lat_v.at[b, mine(c)], 1 + b) for b in range(requests)]
    load_late = [
        load(vup_hbm.at[h], vup_v.at[:, h * value_w : (h + 1) * value_w], 1 + requests + h)
        for h in range(heads)
    ]
    load_late.append(
        load(outw_hbm.at[:, columns(c)], outw_v.at[w_rows(c), :half], 1 + requests + heads)
    )
    if outw_v.shape[1] > half:
        outw_v[:, half:] = jnp.zeros((outw_v.shape[0], outw_v.shape[1] - half), BF16)

    pl.semaphore_wait(barrier, chips)

    others = pl.ds(0, chips - 1)

    def sent(ref, sem):
        remote(ref, ref, sem, sem, partner).wait_send()

    def received(ref, sem):
        remote(ref, ref, sem, sem, partner).wait_recv()

    def queries(b, at):
        return qbuf.at[b, at] if b == 0 else qbuf.at[b, at, :, :lat_w]

    def lat_copy(b, side):
        return remote(lat_hbm.at[b], lat_v.at[b, mine(side)], kvs.at[b], kvr.at[b], partner)

    def crope_copy(side):
        return remote(
            crope_hbm, crope_v.at[:, :, mine(side)], kvs.at[requests], kvr.at[requests], partner
        )

    def w_copy(side):
        return remote(
            outw_hbm.at[:, columns(1 - c)], outw_v.at[w_rows(side), :half],
            kvs.at[requests + 1], kvr.at[requests + 1], partner,
        )

    def send_queries(b, ks):
        for k in ks:
            ref = queries(b, chip)
            remote(ref, ref, qs.at[b], qr.at[b], peer(k) * 2 + c).start()

    send_queries(0, far_first)
    crope_copy(c).start()
    for b in range(requests):
        lat_copy(b, c).start()
    crope_copy(1 - c).wait_recv()

    @pl.when(c == 1)
    def _():
        received(queries(0, others), qr.at[0])

    for b in range(1, requests):
        send_queries(b, far_first)

    @pl.when(c != 1)
    def _():
        received(queries(0, others), qr.at[0])

    first_key = chip * chip_keys
    per_request = chips * block_rows
    tiles = per_request // tile
    tile_chips = tile // block_rows
    lane = lax.broadcasted_iota(jnp.int32, (tile, 128), 1)

    def attend(b, d0):
        query = qbuf[b, pl.ds(d0, tile_chips), :, :lat_w].reshape(tile, lat_w)
        rope_at = lat_w + b * rope_w
        rope = qbuf[0, pl.ds(d0, tile_chips), :, rope_at : rope_at + rope_w].reshape(tile, rope_w)
        row = lax.broadcasted_iota(jnp.int32, (tile, 1), 0) % stretch
        limit = len_s[b] + row - first_key
        peak = None
        for at in range(0, chip_keys, chunk):
            if at == keys:
                if tiles == 1:
                    lat_copy(b, 1 - c).wait_recv()
            span = slice(at, at + chunk)
            begin = (at + c * keys) % chip_keys
            keyed = pl.ds(pl.multiple_of(begin, chunk), chunk)
            raw = lax.dot_general(query, lat_v[b, keyed], NT, preferred_element_type=F32)
            raw = raw + jnp.dot(rope, crope_v[b, :, keyed], preferred_element_type=F32)
            where_key = lax.broadcasted_iota(jnp.int32, (tile, chunk), 1) + begin
            raw = jnp.where(where_key <= limit, raw, masked_score)
            score_s[:, span] = raw
            high = jnp.max(raw, axis=1, keepdims=True)
            peak = high if peak is None else jnp.maximum(peak, high)
        total, pooled = None, None
        for at in range(0, chip_keys, chunk):
            span = slice(at, at + chunk)
            begin = (at + c * keys) % chip_keys
            keyed = pl.ds(pl.multiple_of(begin, chunk), chunk)
            weights = jnp.exp2((score_s[:, span] - peak) * scale2)
            part = jnp.sum(weights, axis=1, keepdims=True)
            pool = jnp.dot(weights.astype(BF16), lat_v[b, keyed], preferred_element_type=F32)
            total = part if total is None else total + part
            pooled = pool if pooled is None else pooled + pool
        stat = jnp.transpose(jnp.where(lane == 0, peak, total))
        stat_b[b, chip, :, pl.ds(pl.multiple_of(d0 * block_rows, 128), tile)] = stat[:2]
        to = pl.ds(d0, tile_chips)
        sb[b, to] = pooled.astype(BF16).reshape(tile_chips, block_rows, lat_w)
        pool_s[b, to] = pooled.reshape(tile_chips, block_rows, lat_w)

    for b in range(requests):
        load_lat[b].wait()
        if b == 0:
            load_crope.wait()
        if b:
            received(queries(b, others), qr.at[b])
        if tiles > 1:
            lat_copy(b, 1 - c).wait_recv()
        if tiles == 1:
            attend(b, 0)
        else:
            def step(t, carry, b=b):
                attend(b, t * tile_chips)
                return carry
            lax.fori_loop(0, tiles, step, 0)
        sent(queries(b, others), qs.at[b])
        for k in far_first:
            ref = stat_b.at[b, chip]
            remote(ref, ref, ts.at[b], tr.at[b], peer(k) * 2 + c).start()
        for k in far_first:
            remote(
                sb.at[b, peer(k)], rb.at[b, chip], qs.at[b], pr.at[b], peer(k) * 2 + c
            ).start()
        if b == 0:
            w_copy(c).start()

    def hv_copy(b, side):
        return remote(hvbuf.at[b, side], hvbuf.at[b, side], qs.at[b], hr.at[b], partner)

    def combine(b):
        received(stat_b.at[b, others], tr.at[b])
        peaks, totals = stat_b[b, :, 0, :], stat_b[b, :, 1, :]
        factors = jnp.exp2((peaks - jnp.max(peaks, axis=0, keepdims=True)) * scale2)
        factors = factors / jnp.sum(factors * totals, axis=0, keepdims=True)
        factors = jnp.concatenate([factors, jnp.zeros((128 - chips, per_request), F32)], axis=0)
        for at in range(0, per_request, 128):
            turn_s[at : at + 128] = jnp.transpose(factors[:, at : at + 128])
        mine = turn_s[pl.ds(pl.multiple_of(chip * block_rows, block_rows), block_rows)]
        lane = lax.broadcasted_iota(jnp.int32, (block_rows, 128), 1)

        def factor(at):
            return jnp.sum(jnp.where(lane == at, mine, 0.0), axis=1, keepdims=True)

        weight = [factor(peer(k)) for k in near_first]
        attended = factor(chip) * pool_s[b, chip]
        received(rb.at[b, others], pr.at[b])
        for i, k in enumerate(near_first):
            attended = attended + weight[i] * rb[b, peer(k)].astype(F32)
        attended = attended.astype(BF16)
        sent(stat_b.at[b, others], ts.at[b])
        values = jnp.dot(attended, vup_v[...], preferred_element_type=F32)
        hvbuf[b, c] = jnp.concatenate(
            [
                values[h * stretch : (h + 1) * stretch, h * value_w : (h + 1) * value_w]
                for h in range(heads)
            ],
            axis=1,
        ).astype(BF16)
        sent(sb.at[b, others], qs.at[b])
        hv_copy(b, c).start()

    upper = chip // (chips // 2)

    def far_owner(i):
        return (owners - 1 - i) * (1 - upper) + i * upper

    def out_copy(b, o):
        return remote(
            ob.at[b, o], orb.at[b, chip], os.at[b], orr.at[b], (base + o) * 2 + c
        )

    def project(b):
        hv_copy(b, 1 - c).wait_recv()
        head_values = jnp.concatenate([hvbuf[b, 0], hvbuf[b, 1]], axis=1)
        for i in range(owners):
            o = far_owner(i)
            at = pl.ds(pl.multiple_of(o * width, 128), width)
            piece = jnp.dot(head_values, outw_v[:, at], preferred_element_type=F32)
            opart[b, o] = piece
            ob[b, o] = piece.astype(BF16)

            @pl.when(chip != base + o)
            def _():
                out_copy(b, o).start()

    is_owner = jnp.logical_and(chip >= base, chip < base + owners)

    def fin_copy(b, o, k):
        ref = fin.at[b, c, o]
        return remote(ref, ref, fs.at[b], fr.at[b], peer(k) * 2 + c)

    def relay_copy(b, side):
        ref = fin.at[b, side]
        return remote(ref, ref, gs.at[b], gr.at[b], partner)

    def reduce_out(b):
        @pl.when(is_owner)
        def _():
            o = chip - base
            received(orb.at[b, others], orr.at[b])
            summed = opart[b, o]
            for k in near_first:
                summed = summed + orb[b, peer(k)].astype(F32)
            fin[b, c, o] = summed.astype(BF16)
            for k in far_first:
                fin_copy(b, o, k).start()

    def by_role(wait):
        if owners > 1:
            @pl.when(is_owner)
            def _():
                wait(pl.ds(0, owners - 1))

        @pl.when(jnp.logical_not(is_owner))
        def _():
            wait(pl.ds(0, owners))

    def place(side):
        for core in range(2):
            @pl.when(side == core)
            def _():
                for o in range(owners):
                    used = min(width, half - o * width)
                    if used > 0:
                        at = core * half + o * width
                        out_ref[:, at : at + used] = jnp.concatenate(
                            [fin[b, core, o, :, :used].astype(F32) for b in range(requests)],
                            axis=0,
                        ).astype(BF16)

    for copy in load_late:
        copy.wait()
    for b in range(requests):
        combine(b)
        if b == 0:
            w_copy(1 - c).wait_recv()
        project(b)
    for b in range(requests):
        reduce_out(b)
    crope_copy(c).wait_send()
    for b in range(requests):
        lat_copy(b, c).wait_send()
        sent(hvbuf.at[b, c], qs.at[b])
        by_role(lambda part: sent(ob.at[b, part], os.at[b]))
    w_copy(c).wait_send()
    for b in range(requests):
        by_role(lambda part: received(fin.at[b, c, part], fr.at[b]))
        relay_copy(b, c).start()
    place(c)

    @pl.when(is_owner)
    def _():
        for b in range(requests):
            sent(orb.at[b, others], fs.at[b])

    for b in range(requests):
        relay_copy(b, 1 - c).wait_recv()
    place(1 - c)
    for b in range(requests):
        relay_copy(b, c).wait_send()


def local(
    n, query_input, query_gain, nope_weight, rope_weight, key_up, value_up, out_weight,
    cache_latent, cache_rope, cached_length,
):
    heads, _, lat_w = key_up.shape
    value_w = value_up.shape[2]
    rows = query_input.shape[0]
    requests, keys, _ = cache_latent.shape
    rope_w = rope_weight.shape[1] // heads
    stretch = rows // requests
    block_rows = heads * stretch
    model = out_weight.shape[1]
    half = model // 2
    chips = n // 2
    owners = max(1, chips // 2)
    tile = min(128, chips * block_rows)
    chunk = min(512, 2 * keys)
    width = -(-half // (128 * owners)) * 128
    vmem = pltpu.VMEM
    dma = lambda *count: pltpu.SemaphoreType.DMA(count)
    any_spec = pl.BlockSpec(memory_space=pl.ANY)
    per_block = (requests, chips, block_rows)
    return pl.pallas_call(
        functools.partial(kernel, n, tile, chunk),
        out_shape=jax.ShapeDtypeStruct((rows, model), BF16),
        in_specs=[any_spec] * 10,
        out_specs=pl.BlockSpec(memory_space=pltpu.VMEM),
        scratch_shapes=[
            vmem(query_input.shape, BF16), vmem(query_gain.shape, BF16),
            vmem(nope_weight.shape, BF16), vmem(rope_weight.shape, BF16),
            vmem(key_up.shape, BF16), vmem((lat_w, heads * value_w), BF16),
            vmem((2 * out_weight.shape[0], owners * width), BF16),
            vmem((requests, 2 * keys, lat_w), BF16),
            vmem((requests, rope_w, 2 * keys), BF16),
            pltpu.SMEM(cached_length.shape, jnp.int32),
            vmem((*per_block, lat_w + requests * rope_w), BF16),
            vmem((tile, 2 * keys), F32),
            vmem((requests, chips, 2, chips * block_rows), F32),
            vmem((chips * block_rows, 128), F32), vmem((*per_block, lat_w), F32),
            vmem((*per_block, lat_w), BF16), vmem((*per_block, lat_w), BF16),
            vmem((requests, 2, stretch, heads * value_w), BF16),
            vmem((requests, owners, stretch, width), F32),
            vmem((requests, owners, stretch, width), BF16),
            vmem((requests, chips, stretch, width), BF16),
            vmem((requests, 2, owners, stretch, width), BF16),
            dma(max(6, 2 + requests + heads)), dma(requests + 2), dma(requests + 2),
            *[dma(requests)] * 12,
        ],
        compiler_params=pltpu.CompilerParams(
            collective_id=0, has_side_effects=True, vmem_limit_bytes=40 * 1024 * 1024
        ),
    )(*[
        pltpu.with_memory_space_constraint(array, pltpu.HBM)
        for array in (
            query_input, query_gain, nope_weight, rope_weight, key_up,
            value_up, out_weight, cache_latent, cache_rope, cached_length,
        )
    ])


def solution(mesh):
    placed = (
        P("groups", None),
        P(),
        P(None, "ctx"),
        P(None, "ctx"),
        P("ctx", None, None),
        P("ctx", None, None),
        P("ctx", None),
        P("groups", "ctx", None),
        P("groups", None, "ctx"),
        P("groups"),
    )
    return jax.shard_map(
        functools.partial(local, mesh.shape["ctx"]), mesh=mesh, in_specs=placed,
        out_specs=P("groups", None), check_vma=False,
    )
```

```python
import functools
import math

import jax
import jax.numpy as jnp
from jax import lax
from jax.experimental import pallas as pl
from jax.experimental.pallas import tpu as pltpu
from jax.sharding import PartitionSpec as P

mscale_yarn = 1.0 + 0.1 * math.log(40.0)
masked_score = -1e30
MESH = pl.DeviceIdType.MESH
F32 = jnp.float32
BF16 = jnp.bfloat16
NT = (((1,), (1,)), ((), ()))


def kernel(
    n, tile, chunk,
    x_hbm, gain_hbm, nope_hbm, ropew_hbm, kup_hbm, vup_hbm, outw_hbm, lat_hbm, crope_hbm, len_hbm,
    out_ref,
    x_v, gain_v, nope_v, ropew_v, kup_v, vup_v, outw_v, lat_v, crope_v, len_s,
    qown, qbuf, score_s, stat_b, turn_s, pool_s, sb, rb, opart, ob, orb, fin,
    ld_sem, kvs, kvr, qs, qr, ts, tr, pr, os, orr, fs, fr, gs, gr,
):
    me = lax.axis_index("ctx")
    chips = n // 2
    chip, c = me // 2, me % 2
    heads, nope_w, lat_w = kup_v.shape
    value_w = vup_hbm.shape[2]
    rows = x_v.shape[0]
    requests, keys, _ = lat_hbm.shape
    chip_keys = 2 * keys
    model = out_ref.shape[1]
    stretch = rows // requests
    block_rows = heads * stretch
    rope_w = ropew_v.shape[1] // heads
    q_w = qbuf.shape[3]
    owners = opart.shape[1]
    base = (chips - owners) // 2
    width = opart.shape[3]
    scale = mscale_yarn * mscale_yarn / math.sqrt(nope_w + rope_w)
    scale2 = scale * math.log2(math.e)
    partner = chip * 2 + 1 - c

    def peer(k):
        flipped, bit = 0, 1
        while bit < chips:
            flipped = flipped + ((chip // bit + (k // bit) % 2) % 2) * bit
            bit *= 2
        return flipped

    near_first = sorted(range(1, chips), key=lambda k: (bin(k).count("1"), k))
    far_first = near_first[::-1]

    def remote(src, dst, ssem, rsem, target):
        return pltpu.make_async_remote_copy(
            src_ref=src, dst_ref=dst, send_sem=ssem, recv_sem=rsem,
            device_id={"ctx": target}, device_id_type=MESH,
        )

    def load(src, dst, slot):
        copy = pltpu.make_async_copy(src, dst, ld_sem.at[slot])
        copy.start()
        return copy

    barrier = pltpu.get_barrier_semaphore()
    load_x = load(x_hbm, x_v, 0)
    load_gain = load(gain_hbm, gain_v, 1)
    load_nope = load(nope_hbm, nope_v, 2)
    load_rope = load(ropew_hbm, ropew_v, 3)
    load_kup = load(kup_hbm, kup_v, 4)
    load_len = load(len_hbm, len_s, 5)
    for k in far_first:
        pl.semaphore_signal(
            barrier, inc=1, device_id={"ctx": peer(k) * 2 + 1 - c}, device_id_type=MESH
        )
    pl.semaphore_signal(barrier, inc=1, device_id={"ctx": partner}, device_id_type=MESH)

    load_x.wait()
    load_gain.wait()
    widened = x_v[...].astype(F32)
    normed = (
        widened
        * lax.rsqrt(jnp.mean(widened * widened, axis=-1, keepdims=True) + 1e-06)
        * gain_v[...].astype(F32).reshape(1, -1)
    ).astype(BF16)
    load_nope.wait()
    load_rope.wait()
    load_kup.wait()
    load_len.wait()
    query_nope = jnp.dot(normed, nope_v[...], preferred_element_type=F32).astype(BF16)
    query_rope = jnp.dot(normed, ropew_v[...], preferred_element_type=F32)

    latents = [
        jnp.dot(
            query_nope[:, h * nope_w : (h + 1) * nope_w], kup_v[h], preferred_element_type=F32
        )
        for h in range(heads)
    ]
    for b in range(requests):
        part = slice(b * stretch, (b + 1) * stretch)
        qown[b, :, :lat_w] = jnp.concatenate([t[part] for t in latents], axis=0).astype(BF16)
    qown[0, :, lat_w:] = jnp.concatenate(
        [
            jnp.concatenate(
                [
                    query_rope[b * stretch : (b + 1) * stretch, h * rope_w : (h + 1) * rope_w]
                    for b in range(requests)
                ],
                axis=1,
            )
            for h in range(heads)
        ],
        axis=0,
    ).astype(BF16)
    mine = lambda at: pl.ds(pl.multiple_of(at * keys, 128), keys)
    out_rows = outw_hbm.shape[0]
    load_crope = load(crope_hbm, crope_v.at[:, :, mine(c)], 0)
    load_lat = [load(lat_hbm.at[b], lat_v.at[b, mine(c)], 1 + b) for b in range(requests)]
    if outw_v.shape[1] > model:
        outw_v[:, model:] = jnp.zeros((outw_v.shape[0], outw_v.shape[1] - model), BF16)

    def late_refs(side):
        pairs = [
            (vup_hbm.at[h], vup_v.at[side, :, h * value_w : (h + 1) * value_w])
            for h in range(heads)
        ]
        cut = out_rows // 2
        return [
            *pairs,
            (outw_hbm.at[:cut], outw_v.at[side * out_rows : side * out_rows + cut, :model]),
            (outw_hbm.at[cut:], outw_v.at[side * out_rows + cut : (side + 1) * out_rows, :model]),
        ]

    def late_loads():
        return [
            pltpu.make_async_copy(src, dst, ld_sem.at[1 + requests + i])
            for i, (src, dst) in enumerate(late_refs(1))
        ]

    @pl.when(c == 1)
    def _():
        for copy in late_loads():
            copy.start()

    pl.semaphore_wait(barrier, chips)

    others, everyone = pl.ds(0, chips - 1), pl.ds(0, chips)
    group = 1 - c

    def sent(ref, sem):
        remote(ref, ref, sem, sem, partner).wait_send()

    def received(ref, sem):
        remote(ref, ref, sem, sem, partner).wait_recv()

    def queries(b, at):
        return qbuf.at[b, at] if b == 0 else qbuf.at[b, at, :, :lat_w]

    def lat_copy(b, side):
        return remote(lat_hbm.at[b], lat_v.at[b, mine(side)], kvs.at[b], kvr.at[b], partner)

    def crope_copy(side):
        return remote(
            crope_hbm, crope_v.at[:, :, mine(side)], kvs.at[requests], kvr.at[requests], partner
        )

    def late_copies():
        return [
            remote(
                src, dst, kvs.at[requests + 1 + i], kvr.at[requests + 1 + i], partner
            )
            for i, (src, dst) in enumerate(late_refs(0))
        ]

    def send_queries(b, ks):
        for k in ks:
            src = qown.at[b] if b == 0 else qown.at[b, :, :lat_w]
            remote(src, queries(b, chip), qs.at[b], qr.at[b], peer(k) * 2 + 1 - c).start()

    send_queries(0, [*far_first, 0])
    crope_copy(c).start()
    for b in range(requests):
        lat_copy(b, c).start()
    crope_copy(1 - c).wait_recv()

    @pl.when(c == 1)
    def _():
        lat_copy(0, 1 - c).wait_recv()

    for b in range(1, requests):
        send_queries(b, [*far_first, 0])
    received(queries(0, everyone), qr.at[0])

    @pl.when(c != 1)
    def _():
        lat_copy(0, 1 - c).wait_recv()

    @pl.when(c == 0)
    def _():
        for copy in late_copies()[:4]:
            copy.start()

    first_key = chip * chip_keys
    per_request = chips * block_rows
    tiles = per_request // tile
    tile_chips = tile // block_rows
    lane = lax.broadcasted_iota(jnp.int32, (tile, 128), 1)

    def attend(b, d0):
        query = qbuf[b, pl.ds(d0, tile_chips), :, :lat_w].reshape(tile, lat_w)
        rope_at = lat_w + b * rope_w
        rope = qbuf[0, pl.ds(d0, tile_chips), :, rope_at : rope_at + rope_w].reshape(tile, rope_w)
        row = lax.broadcasted_iota(jnp.int32, (tile, 1), 0) % stretch
        limit = len_s[b] + row - first_key
        peak = None
        for at in range(0, chip_keys, chunk):
            if at == keys:
                if tiles == 1 and b:
                    lat_copy(b, 1 - c).wait_recv()
            span = slice(at, at + chunk)
            begin = (at + c * keys) % chip_keys
            keyed = pl.ds(pl.multiple_of(begin, chunk), chunk)
            raw = lax.dot_general(query, lat_v[b, keyed], NT, preferred_element_type=F32)
            raw = raw + jnp.dot(rope, crope_v[b, :, keyed], preferred_element_type=F32)
            where_key = lax.broadcasted_iota(jnp.int32, (tile, chunk), 1) + begin
            raw = jnp.where(where_key <= limit, raw, masked_score)
            score_s[:, span] = raw
            high = jnp.max(raw, axis=1, keepdims=True)
            peak = high if peak is None else jnp.maximum(peak, high)
        total, pooled = None, None
        for at in range(0, chip_keys, chunk):
            span = slice(at, at + chunk)
            begin = (at + c * keys) % chip_keys
            keyed = pl.ds(pl.multiple_of(begin, chunk), chunk)
            weights = jnp.exp2((score_s[:, span] - peak) * scale2)
            part = jnp.sum(weights, axis=1, keepdims=True)
            pool = jnp.dot(weights.astype(BF16), lat_v[b, keyed], preferred_element_type=F32)
            total = part if total is None else total + part
            pooled = pool if pooled is None else pooled + pool
        stat = jnp.transpose(jnp.where(lane == 0, peak, total))
        stat_b[b, group * chips + chip, :, pl.ds(pl.multiple_of(d0 * block_rows, 128), tile)] = stat[:2]
        to = pl.ds(d0, tile_chips)
        sb[b, to] = pooled.astype(BF16).reshape(tile_chips, block_rows, lat_w)
        pool_s[b, to] = pooled.reshape(tile_chips, block_rows, lat_w)

    def pool_copy(b, k):
        return remote(
            sb.at[b, peer(k)], rb.at[b, group * chips + chip], qs.at[b], pr.at[b],
            peer(k) * 2 + 1,
        )

    for b in range(requests):
        load_lat[b].wait()
        if b == 0:
            load_crope.wait()
        if b:
            received(queries(b, everyone), qr.at[b])
        if tiles > 1 and b:
            lat_copy(b, 1 - c).wait_recv()
        if tiles == 1:
            attend(b, 0)
        else:
            def step(t, carry, b=b):
                attend(b, t * tile_chips)
                return carry
            lax.fori_loop(0, tiles, step, 0)
        sent(queries(b, everyone), qs.at[b])
        for k in far_first:
            ref = stat_b.at[b, group * chips + chip]
            remote(ref, ref, ts.at[b], tr.at[b], peer(k) * 2 + 1).start()
        for k in far_first:
            pool_copy(b, k).start()

        @pl.when(c == 0)
        def _():
            ref = stat_b.at[b, group * chips + chip]
            remote(ref, ref, ts.at[b], tr.at[b], partner).start()
            pool_copy(b, 0).start()
            if b == 0:
                for copy in late_copies()[4:]:
                    copy.start()

    def combine(b):
        received(stat_b.at[b, pl.ds(0, 2 * chips - 1)], tr.at[b])
        weight = []
        for g in range(2):
            at_chips = slice(g * chips, (g + 1) * chips)
            peaks, totals = stat_b[b, at_chips, 0, :], stat_b[b, at_chips, 1, :]
            factors = jnp.exp2((peaks - jnp.max(peaks, axis=0, keepdims=True)) * scale2)
            factors = factors / jnp.sum(factors * totals, axis=0, keepdims=True)
            factors = jnp.concatenate(
                [factors, jnp.zeros((128 - chips, per_request), F32)], axis=0
            )
            for at in range(0, per_request, 128):
                turn_s[g, at : at + 128] = jnp.transpose(factors[:, at : at + 128])
            mine = turn_s[g, pl.ds(pl.multiple_of(chip * block_rows, block_rows), block_rows)]
            lane = lax.broadcasted_iota(jnp.int32, (block_rows, 128), 1)
            weight.append([
                jnp.sum(jnp.where(lane == peer(k), mine, 0.0), axis=1, keepdims=True)
                for k in range(chips)
            ])
        received(rb.at[b, pl.ds(0, 2 * chips - 1)], pr.at[b])
        head_values = []
        for g in range(2):
            attended = 0.0
            for k in range(chips):
                if g == 0 and k == 0:
                    pooled = pool_s[b, chip]
                else:
                    pooled = rb[b, g * chips + peer(k)].astype(F32)
                attended = attended + weight[g][k] * pooled
            values = jnp.dot(attended.astype(BF16), vup_v[g], preferred_element_type=F32)
            for h in range(heads):
                head_values.append(
                    values[h * stretch : (h + 1) * stretch, h * value_w : (h + 1) * value_w]
                )
        return jnp.concatenate(head_values, axis=1).astype(BF16)

    upper = chip // (chips // 2)

    def far_owner(i):
        return (owners - 1 - i) * (1 - upper) + i * upper

    def out_copy(b, o):
        return remote(
            ob.at[b, o], orb.at[b, chip], os.at[b], orr.at[b], (base + o) * 2 + 1
        )

    def project(b, head_values):
        for i in range(owners):
            o = far_owner(i)
            at = pl.ds(pl.multiple_of(o * width, 128), width)
            piece = jnp.dot(head_values, outw_v[:, at], preferred_element_type=F32)
            opart[b, o] = piece
            ob[b, o] = piece.astype(BF16)

            @pl.when(chip != base + o)
            def _():
                out_copy(b, o).start()

    is_owner = jnp.logical_and(chip >= base, chip < base + owners)

    def fin_copy(b, o, k):
        ref = fin.at[b, o]
        return remote(ref, ref, fs.at[b], fr.at[b], peer(k) * 2 + 1)

    def relay_copy(b):
        return remote(fin.at[b], fin.at[b], gs.at[b], gr.at[b], partner)

    def reduce_out(b):
        @pl.when(is_owner)
        def _():
            o = chip - base
            received(orb.at[b, others], orr.at[b])
            summed = opart[b, o]
            for k in near_first:
                summed = summed + orb[b, peer(k)].astype(F32)
            fin[b, o] = summed.astype(BF16)
            for k in far_first:
                fin_copy(b, o, k).start()

    def by_role(wait):
        if owners > 1:
            @pl.when(is_owner)
            def _():
                wait(pl.ds(0, owners - 1))

        @pl.when(jnp.logical_not(is_owner))
        def _():
            wait(pl.ds(0, owners))

    def place():
        for o in range(owners):
            used = min(width, model - o * width)
            if used > 0:
                at = o * width
                out_ref[:, at : at + used] = jnp.concatenate(
                    [fin[b, o, :, :used].astype(F32) for b in range(requests)], axis=0
                ).astype(BF16)

    def finish_queries():
        crope_copy(c).wait_send()
        for b in range(requests):
            lat_copy(b, c).wait_send()

    @pl.when(c == 0)
    def _():
        finish_queries()
        for copy in late_copies():
            copy.wait_send()
        for b in range(requests):
            sent(stat_b.at[b, everyone], ts.at[b])
            sent(sb.at[b, everyone], qs.at[b])
        for b in range(requests):
            relay_copy(b).wait_recv()
        place()

    @pl.when(c == 1)
    def _():
        for copy in late_loads():
            copy.wait()
        for copy in late_copies()[:heads]:
            copy.wait_recv()
        for b in range(requests):
            head_values = combine(b)
            if b == 0:
                for copy in late_copies()[heads:]:
                    copy.wait_recv()
            project(b, head_values)
        finish_queries()
        for b in range(requests):
            reduce_out(b)
        for b in range(requests):
            sent(stat_b.at[b, others], ts.at[b])
            sent(sb.at[b, others], qs.at[b])
            by_role(lambda part: sent(ob.at[b, part], os.at[b]))
        for b in range(requests):
            by_role(lambda part: received(fin.at[b, part], fr.at[b]))
            relay_copy(b).start()
        place()

        @pl.when(is_owner)
        def _():
            for b in range(requests):
                sent(orb.at[b, others], fs.at[b])

        for b in range(requests):
            relay_copy(b).wait_send()


def local(
    n, query_input, query_gain, nope_weight, rope_weight, key_up, value_up, out_weight,
    cache_latent, cache_rope, cached_length,
):
    heads, _, lat_w = key_up.shape
    value_w = value_up.shape[2]
    rows = query_input.shape[0]
    requests, keys, _ = cache_latent.shape
    rope_w = rope_weight.shape[1] // heads
    stretch = rows // requests
    block_rows = heads * stretch
    model = out_weight.shape[1]
    chips = n // 2
    owners = max(1, chips // 2)
    tile = min(128, chips * block_rows)
    chunk = min(512, 2 * keys)
    width = -(-model // (128 * owners)) * 128
    vmem = pltpu.VMEM
    dma = lambda *count: pltpu.SemaphoreType.DMA(count)
    any_spec = pl.BlockSpec(memory_space=pl.ANY)
    per_block = (requests, chips, block_rows)
    return pl.pallas_call(
        functools.partial(kernel, n, tile, chunk),
        out_shape=jax.ShapeDtypeStruct((rows, model), BF16),
        in_specs=[any_spec] * 10,
        out_specs=pl.BlockSpec(memory_space=pltpu.VMEM),
        scratch_shapes=[
            vmem(query_input.shape, BF16), vmem(query_gain.shape, BF16),
            vmem(nope_weight.shape, BF16), vmem(rope_weight.shape, BF16),
            vmem(key_up.shape, BF16), vmem((2, lat_w, heads * value_w), BF16),
            vmem((2 * out_weight.shape[0], owners * width), BF16),
            vmem((requests, 2 * keys, lat_w), BF16),
            vmem((requests, rope_w, 2 * keys), BF16),
            pltpu.SMEM(cached_length.shape, jnp.int32),
            vmem((requests, block_rows, lat_w + requests * rope_w), BF16),
            vmem((*per_block, lat_w + requests * rope_w), BF16),
            vmem((tile, 2 * keys), F32),
            vmem((requests, 2 * chips, 2, chips * block_rows), F32),
            vmem((2, chips * block_rows, 128), F32), vmem((*per_block, lat_w), F32),
            vmem((*per_block, lat_w), BF16), vmem((requests, 2 * chips, block_rows, lat_w), BF16),
            vmem((requests, owners, stretch, width), F32),
            vmem((requests, owners, stretch, width), BF16),
            vmem((requests, chips, stretch, width), BF16),
            vmem((requests, owners, stretch, width), BF16),
            dma(max(6, 3 + requests + heads)), dma(requests + 3 + heads), dma(requests + 3 + heads),
            *[dma(requests)] * 11,
        ],
        compiler_params=pltpu.CompilerParams(
            collective_id=0, has_side_effects=True, vmem_limit_bytes=40 * 1024 * 1024
        ),
    )(*[
        pltpu.with_memory_space_constraint(array, pltpu.HBM)
        for array in (
            query_input, query_gain, nope_weight, rope_weight, key_up,
            value_up, out_weight, cache_latent, cache_rope, cached_length,
        )
    ])


def solution(mesh):
    placed = (
        P("groups", None),
        P(),
        P(None, "ctx"),
        P(None, "ctx"),
        P("ctx", None, None),
        P("ctx", None, None),
        P("ctx", None),
        P("groups", "ctx", None),
        P("groups", None, "ctx"),
        P("groups"),
    )
    return jax.shard_map(
        functools.partial(local, mesh.shape["ctx"]), mesh=mesh, in_specs=placed,
        out_specs=P("groups", None), check_vma=False,
    )
```

```python
import functools
import math

import jax
import jax.numpy as jnp
from jax import lax
from jax.experimental import pallas as pl
from jax.experimental.pallas import tpu as pltpu
from jax.sharding import PartitionSpec as P

mscale_yarn = 1.0 + 0.1 * math.log(40.0)
masked_score = -1e30
MESH = pl.DeviceIdType.MESH
F32 = jnp.float32
BF16 = jnp.bfloat16
NT = (((1,), (1,)), ((), ()))


def kernel(
    n, tile, chunk,
    x_hbm, gain_hbm, nope_hbm, ropew_hbm, kup_hbm, vup_hbm, outw_hbm, lat_hbm, crope_hbm, len_hbm,
    out_ref,
    x_v, gain_v, nope_v, ropew_v, kup_v, vup_v, outw_v, lat_v, crope_v, len_s,
    qown, qbuf, score_s, stat_b, turn_s, pool_s, sb, rb, opart, ob, orb, fin,
    ld_sem, kvs, kvr, qs, qr, ts, tr, pr, os, orr, fs, fr, gs, gr,
):
    me = lax.axis_index("ctx")
    chips = n // 2
    chip, c = me // 2, me % 2
    heads, nope_w, lat_w = kup_v.shape
    value_w = vup_hbm.shape[2]
    rows = x_v.shape[0]
    requests, keys, _ = lat_hbm.shape
    chip_keys = 2 * keys
    model = out_ref.shape[1]
    stretch = rows // requests
    block_rows = heads * stretch
    rope_w = ropew_v.shape[1] // heads
    q_w = qbuf.shape[3]
    owners = opart.shape[1]
    base = (chips - owners) // 2
    width = opart.shape[3]
    scale = mscale_yarn * mscale_yarn / math.sqrt(nope_w + rope_w)
    scale2 = scale * math.log2(math.e)
    partner = chip * 2 + 1 - c

    def peer(k):
        flipped, bit = 0, 1
        while bit < chips:
            flipped = flipped + ((chip // bit + (k // bit) % 2) % 2) * bit
            bit *= 2
        return flipped

    near_first = sorted(range(1, chips), key=lambda k: (bin(k).count("1"), k))
    far_first = near_first[::-1]

    def remote(src, dst, ssem, rsem, target):
        return pltpu.make_async_remote_copy(
            src_ref=src, dst_ref=dst, send_sem=ssem, recv_sem=rsem,
            device_id={"ctx": target}, device_id_type=MESH,
        )

    def load(src, dst, slot):
        copy = pltpu.make_async_copy(src, dst, ld_sem.at[slot])
        copy.start()
        return copy

    barrier = pltpu.get_barrier_semaphore()
    load_x = load(x_hbm, x_v, 0)
    load_gain = load(gain_hbm, gain_v, 1)
    load_nope = load(nope_hbm, nope_v, 2)
    load_rope = load(ropew_hbm, ropew_v, 3)
    load_kup = load(kup_hbm, kup_v, 4)
    load_len = load(len_hbm, len_s, 5)
    for k in far_first:
        pl.semaphore_signal(
            barrier, inc=1, device_id={"ctx": peer(k) * 2 + 1 - c}, device_id_type=MESH
        )
    pl.semaphore_signal(barrier, inc=1, device_id={"ctx": partner}, device_id_type=MESH)

    load_x.wait()
    load_gain.wait()
    widened = x_v[...].astype(F32)
    normed = (
        widened
        * lax.rsqrt(jnp.mean(widened * widened, axis=-1, keepdims=True) + 1e-06)
        * gain_v[...].astype(F32).reshape(1, -1)
    ).astype(BF16)
    load_nope.wait()
    load_rope.wait()
    load_kup.wait()
    load_len.wait()
    query_nope = jnp.dot(normed, nope_v[...], preferred_element_type=F32).astype(BF16)
    query_rope = jnp.dot(normed, ropew_v[...], preferred_element_type=F32)

    latents = [
        jnp.dot(
            query_nope[:, h * nope_w : (h + 1) * nope_w], kup_v[h], preferred_element_type=F32
        )
        for h in range(heads)
    ]
    for b in range(requests):
        part = slice(b * stretch, (b + 1) * stretch)
        qown[b, :, :lat_w] = jnp.concatenate([t[part] for t in latents], axis=0).astype(BF16)
    qown[0, :, lat_w:] = jnp.concatenate(
        [
            jnp.concatenate(
                [
                    query_rope[b * stretch : (b + 1) * stretch, h * rope_w : (h + 1) * rope_w]
                    for b in range(requests)
                ],
                axis=1,
            )
            for h in range(heads)
        ],
        axis=0,
    ).astype(BF16)
    mine = lambda at: pl.ds(pl.multiple_of(at * keys, 128), keys)
    out_rows = outw_hbm.shape[0]
    load_crope = load(crope_hbm, crope_v.at[:, :, mine(c)], 0)
    load_lat = [load(lat_hbm.at[b], lat_v.at[b, mine(c)], 1 + b) for b in range(requests)]
    if outw_v.shape[1] > model:
        outw_v[:, model:] = jnp.zeros((outw_v.shape[0], outw_v.shape[1] - model), BF16)

    def late_refs(side):
        pairs = [
            (vup_hbm.at[h], vup_v.at[side, :, h * value_w : (h + 1) * value_w])
            for h in range(heads)
        ]
        cut = out_rows // 2
        return [
            *pairs,
            (outw_hbm.at[:cut], outw_v.at[side * out_rows : side * out_rows + cut, :model]),
            (outw_hbm.at[cut:], outw_v.at[side * out_rows + cut : (side + 1) * out_rows, :model]),
        ]

    def late_loads():
        return [
            pltpu.make_async_copy(src, dst, ld_sem.at[1 + requests + i])
            for i, (src, dst) in enumerate(late_refs(1))
        ]

    @pl.when(c == 1)
    def _():
        for copy in late_loads():
            copy.start()

    pl.semaphore_wait(barrier, chips)

    others, everyone = pl.ds(0, chips - 1), pl.ds(0, chips)
    group = 1 - c

    def sent(ref, sem):
        remote(ref, ref, sem, sem, partner).wait_send()

    def received(ref, sem):
        remote(ref, ref, sem, sem, partner).wait_recv()

    def queries(b, at):
        return qbuf.at[b, at] if b == 0 else qbuf.at[b, at, :, :lat_w]

    def lat_copy(b, side):
        return remote(lat_hbm.at[b], lat_v.at[b, mine(side)], kvs.at[b], kvr.at[b], partner)

    def crope_copy(side):
        return remote(
            crope_hbm, crope_v.at[:, :, mine(side)], kvs.at[requests], kvr.at[requests], partner
        )

    def late_copies():
        return [
            remote(
                src, dst, kvs.at[requests + 1 + i], kvr.at[requests + 1 + i], partner
            )
            for i, (src, dst) in enumerate(late_refs(0))
        ]

    def send_queries(b, ks):
        for k in ks:
            src = qown.at[b] if b == 0 else qown.at[b, :, :lat_w]
            remote(src, queries(b, chip), qs.at[b], qr.at[b], peer(k) * 2 + 1 - c).start()

    send_queries(0, [0, *far_first])
    crope_copy(c).start()
    for b in range(requests):
        lat_copy(b, c).start()
    crope_copy(1 - c).wait_recv()

    @pl.when(c == 1)
    def _():
        lat_copy(0, 1 - c).wait_recv()

    for b in range(1, requests):
        send_queries(b, [*far_first, 0])
    received(queries(0, everyone), qr.at[0])

    @pl.when(c != 1)
    def _():
        lat_copy(0, 1 - c).wait_recv()

    @pl.when(c == 0)
    def _():
        for copy in late_copies()[:4]:
            copy.start()

    first_key = chip * chip_keys
    per_request = chips * block_rows
    tiles = per_request // tile
    tile_chips = tile // block_rows
    lane = lax.broadcasted_iota(jnp.int32, (tile, 128), 1)

    def attend(b, d0):
        query = qbuf[b, pl.ds(d0, tile_chips), :, :lat_w].reshape(tile, lat_w)
        rope_at = lat_w + b * rope_w
        rope = qbuf[0, pl.ds(d0, tile_chips), :, rope_at : rope_at + rope_w].reshape(tile, rope_w)
        row = lax.broadcasted_iota(jnp.int32, (tile, 1), 0) % stretch
        limit = len_s[b] + row - first_key
        peak = None
        for at in range(0, chip_keys, chunk):
            if at == keys:
                if tiles == 1 and b:
                    lat_copy(b, 1 - c).wait_recv()
            span = slice(at, at + chunk)
            begin = (at + c * keys) % chip_keys
            keyed = pl.ds(pl.multiple_of(begin, chunk), chunk)
            raw = lax.dot_general(query, lat_v[b, keyed], NT, preferred_element_type=F32)
            raw = raw + jnp.dot(rope, crope_v[b, :, keyed], preferred_element_type=F32)
            where_key = lax.broadcasted_iota(jnp.int32, (tile, chunk), 1) + begin
            raw = jnp.where(where_key <= limit, raw, masked_score)
            score_s[:, span] = raw
            high = jnp.max(raw, axis=1, keepdims=True)
            peak = high if peak is None else jnp.maximum(peak, high)
        total, pooled = None, None
        for at in range(0, chip_keys, chunk):
            span = slice(at, at + chunk)
            begin = (at + c * keys) % chip_keys
            keyed = pl.ds(pl.multiple_of(begin, chunk), chunk)
            weights = jnp.exp2((score_s[:, span] - peak) * scale2)
            part = jnp.sum(weights, axis=1, keepdims=True)
            pool = jnp.dot(weights.astype(BF16), lat_v[b, keyed], preferred_element_type=F32)
            total = part if total is None else total + part
            pooled = pool if pooled is None else pooled + pool
        stat = jnp.transpose(jnp.where(lane == 0, peak, total))
        stat_b[b, group * chips + chip, :, pl.ds(pl.multiple_of(d0 * block_rows, 128), tile)] = stat[:2]
        to = pl.ds(d0, tile_chips)
        sb[b, to] = pooled.astype(BF16).reshape(tile_chips, block_rows, lat_w)
        pool_s[b, to] = pooled.reshape(tile_chips, block_rows, lat_w)

    def pool_copy(b, k):
        return remote(
            sb.at[b, peer(k)], rb.at[b, group * chips + chip], qs.at[b], pr.at[b],
            peer(k) * 2 + 1,
        )

    for b in range(requests):
        load_lat[b].wait()
        if b == 0:
            load_crope.wait()
        if b:
            received(queries(b, everyone), qr.at[b])
        if tiles > 1 and b:
            lat_copy(b, 1 - c).wait_recv()
        if tiles == 1:
            attend(b, 0)
        else:
            def step(t, carry, b=b):
                attend(b, t * tile_chips)
                return carry
            lax.fori_loop(0, tiles, step, 0)
        sent(queries(b, everyone), qs.at[b])
        for k in near_first:
            ref = stat_b.at[b, group * chips + chip]
            remote(ref, ref, ts.at[b], tr.at[b], peer(k) * 2 + 1).start()
        for k in far_first:
            pool_copy(b, k).start()

        @pl.when(c == 0)
        def _():
            ref = stat_b.at[b, group * chips + chip]
            remote(ref, ref, ts.at[b], tr.at[b], partner).start()
            pool_copy(b, 0).start()
            if b == 0:
                for copy in late_copies()[4:]:
                    copy.start()

    def combine(b):
        received(stat_b.at[b, pl.ds(0, 2 * chips - 1)], tr.at[b])
        weight = []
        for g in range(2):
            at_chips = slice(g * chips, (g + 1) * chips)
            peaks, totals = stat_b[b, at_chips, 0, :], stat_b[b, at_chips, 1, :]
            factors = jnp.exp2((peaks - jnp.max(peaks, axis=0, keepdims=True)) * scale2)
            factors = factors / jnp.sum(factors * totals, axis=0, keepdims=True)
            factors = jnp.concatenate(
                [factors, jnp.zeros((128 - chips, per_request), F32)], axis=0
            )
            for at in range(0, per_request, 128):
                turn_s[g, at : at + 128] = jnp.transpose(factors[:, at : at + 128])
            mine = turn_s[g, pl.ds(pl.multiple_of(chip * block_rows, block_rows), block_rows)]
            lane = lax.broadcasted_iota(jnp.int32, (block_rows, 128), 1)
            weight.append([
                jnp.sum(jnp.where(lane == peer(k), mine, 0.0), axis=1, keepdims=True)
                for k in range(chips)
            ])
        received(rb.at[b, pl.ds(0, 2 * chips - 1)], pr.at[b])
        head_values = []
        for g in range(2):
            attended = 0.0
            for k in range(chips):
                if g == 0 and k == 0:
                    pooled = pool_s[b, chip]
                else:
                    pooled = rb[b, g * chips + peer(k)].astype(F32)
                attended = attended + weight[g][k] * pooled
            values = jnp.dot(attended.astype(BF16), vup_v[g], preferred_element_type=F32)
            for h in range(heads):
                head_values.append(
                    values[h * stretch : (h + 1) * stretch, h * value_w : (h + 1) * value_w]
                )
        return jnp.concatenate(head_values, axis=1).astype(BF16)

    upper = chip // (chips // 2)

    def far_owner(i):
        return (owners - 1 - i) * (1 - upper) + i * upper

    def out_copy(b, o):
        return remote(
            ob.at[b, o], orb.at[b, chip], os.at[b], orr.at[b], (base + o) * 2 + 1
        )

    def project(b, head_values):
        for i in range(owners):
            o = far_owner(i)
            at = pl.ds(pl.multiple_of(o * width, 128), width)
            piece = jnp.dot(head_values, outw_v[:, at], preferred_element_type=F32)
            opart[b, o] = piece
            ob[b, o] = piece.astype(BF16)

            @pl.when(chip != base + o)
            def _():
                out_copy(b, o).start()

    is_owner = jnp.logical_and(chip >= base, chip < base + owners)

    def fin_copy(b, o, k):
        ref = fin.at[b, o]
        return remote(ref, ref, fs.at[b], fr.at[b], peer(k) * 2 + 1)

    def relay_copy(b):
        return remote(fin.at[b], fin.at[b], gs.at[b], gr.at[b], partner)

    def reduce_out(b):
        @pl.when(is_owner)
        def _():
            o = chip - base
            received(orb.at[b, others], orr.at[b])
            summed = opart[b, o]
            for k in near_first:
                summed = summed + orb[b, peer(k)].astype(F32)
            fin[b, o] = summed.astype(BF16)
            for k in far_first:
                fin_copy(b, o, k).start()

    def by_role(wait):
        if owners > 1:
            @pl.when(is_owner)
            def _():
                wait(pl.ds(0, owners - 1))

        @pl.when(jnp.logical_not(is_owner))
        def _():
            wait(pl.ds(0, owners))

    def place():
        for o in range(owners):
            used = min(width, model - o * width)
            if used > 0:
                at = o * width
                out_ref[:, at : at + used] = jnp.concatenate(
                    [fin[b, o, :, :used].astype(F32) for b in range(requests)], axis=0
                ).astype(BF16)

    def finish_queries():
        crope_copy(c).wait_send()
        for b in range(requests):
            lat_copy(b, c).wait_send()

    @pl.when(c == 0)
    def _():
        finish_queries()
        for copy in late_copies():
            copy.wait_send()
        for b in range(requests):
            sent(stat_b.at[b, everyone], ts.at[b])
            sent(sb.at[b, everyone], qs.at[b])
        for b in range(requests):
            relay_copy(b).wait_recv()
        place()

    @pl.when(c == 1)
    def _():
        for copy in late_loads():
            copy.wait()
        for copy in late_copies()[:heads]:
            copy.wait_recv()
        for b in range(requests):
            head_values = combine(b)
            if b == 0:
                for copy in late_copies()[heads:]:
                    copy.wait_recv()
            project(b, head_values)
        finish_queries()
        for b in range(requests):
            reduce_out(b)
        for b in range(requests):
            sent(stat_b.at[b, others], ts.at[b])
            sent(sb.at[b, others], qs.at[b])
            by_role(lambda part: sent(ob.at[b, part], os.at[b]))
        for b in range(requests):
            by_role(lambda part: received(fin.at[b, part], fr.at[b]))
            relay_copy(b).start()
        place()

        @pl.when(is_owner)
        def _():
            for b in range(requests):
                sent(orb.at[b, others], fs.at[b])

        for b in range(requests):
            relay_copy(b).wait_send()


def local(
    n, query_input, query_gain, nope_weight, rope_weight, key_up, value_up, out_weight,
    cache_latent, cache_rope, cached_length,
):
    heads, _, lat_w = key_up.shape
    value_w = value_up.shape[2]
    rows = query_input.shape[0]
    requests, keys, _ = cache_latent.shape
    rope_w = rope_weight.shape[1] // heads
    stretch = rows // requests
    block_rows = heads * stretch
    model = out_weight.shape[1]
    chips = n // 2
    owners = max(1, chips // 2)
    tile = min(128, chips * block_rows)
    chunk = min(2048, 2 * keys)
    width = -(-model // (128 * owners)) * 128
    vmem = pltpu.VMEM
    dma = lambda *count: pltpu.SemaphoreType.DMA(count)
    any_spec = pl.BlockSpec(memory_space=pl.ANY)
    per_block = (requests, chips, block_rows)
    return pl.pallas_call(
        functools.partial(kernel, n, tile, chunk),
        out_shape=jax.ShapeDtypeStruct((rows, model), BF16),
        in_specs=[any_spec] * 10,
        out_specs=pl.BlockSpec(memory_space=pltpu.VMEM),
        scratch_shapes=[
            vmem(query_input.shape, BF16), vmem(query_gain.shape, BF16),
            vmem(nope_weight.shape, BF16), vmem(rope_weight.shape, BF16),
            vmem(key_up.shape, BF16), vmem((2, lat_w, heads * value_w), BF16),
            vmem((2 * out_weight.shape[0], owners * width), BF16),
            vmem((requests, 2 * keys, lat_w), BF16),
            vmem((requests, rope_w, 2 * keys), BF16),
            pltpu.SMEM(cached_length.shape, jnp.int32),
            vmem((requests, block_rows, lat_w + requests * rope_w), BF16),
            vmem((*per_block, lat_w + requests * rope_w), BF16),
            vmem((tile, 2 * keys), F32),
            vmem((requests, 2 * chips, 2, chips * block_rows), F32),
            vmem((2, chips * block_rows, 128), F32), vmem((*per_block, lat_w), F32),
            vmem((*per_block, lat_w), BF16), vmem((requests, 2 * chips, block_rows, lat_w), BF16),
            vmem((requests, owners, stretch, width), F32),
            vmem((requests, owners, stretch, width), BF16),
            vmem((requests, chips, stretch, width), BF16),
            vmem((requests, owners, stretch, width), BF16),
            dma(max(6, 3 + requests + heads)), dma(requests + 3 + heads), dma(requests + 3 + heads),
            *[dma(requests)] * 11,
        ],
        compiler_params=pltpu.CompilerParams(
            collective_id=0, has_side_effects=True, vmem_limit_bytes=40 * 1024 * 1024
        ),
    )(*[
        pltpu.with_memory_space_constraint(array, pltpu.HBM)
        for array in (
            query_input, query_gain, nope_weight, rope_weight, key_up,
            value_up, out_weight, cache_latent, cache_rope, cached_length,
        )
    ])


def solution(mesh):
    placed = (
        P("groups", None),
        P(),
        P(None, "ctx"),
        P(None, "ctx"),
        P("ctx", None, None),
        P("ctx", None, None),
        P("ctx", None),
        P("groups", "ctx", None),
        P("groups", None, "ctx"),
        P("groups"),
    )
    return jax.shard_map(
        functools.partial(local, mesh.shape["ctx"]), mesh=mesh, in_specs=placed,
        out_specs=P("groups", None), check_vma=False,
    )
```
